32 devices in a mesh: cell: 8 (over z, x), tile: 4 (over y, core).
Axes of the slice: x: 2, y: 2, z: 4, core: 2. Of those that a mesh axis runs over, the one named last changes fastest.
Arguments:
- gaussians: float32 [59, 32768], P(None, 'cell'), as said below
- tile_lists: int32 [8, 32, 256], P('cell', 'tile'), may hold values from 0 to 4095, as said below
- list_blocks: int32 [8, 32], P('cell', 'tile'), may hold values from 1 to 2, as said below
- cell_order: int32 [8], replicated, may hold values from 0 to 7, each once
- view_vector: float32 [3], replicated, may hold values from 0.5 to 1
- cotangent: float32 [3, 32, 256], P(None, 'tile'), may hold values from -6 to 6
Outputs:
- rendered: float32 [3, 32, 256], P(None, 'tile')
- gaussian_grads: float32 [59, 32768], P(None, ('cell', 'tile'))
The draws below stay inside these ranges and needn't reach their ends.
Inputs may be any that keep to these rules, and one draw needn't show every extreme that they name: `gaussians`: Rows: 0-1 center in pixels, 2 depth between 4 and 8, 3-5 log scales, 6-9 a quaternion whose first entry lies between 1 and 2, 10 opacity logit, 11-58 colour coefficients, 16 for each channel in turn. `tile_lists`: indices are local to the cell's block of 4096 Gaussians. Only the first 128 * list_blocks[c,k] entries of the list of cell c and tile k are used; every cell has tiles with the most and the least.
All inputs are finite; a program needn't handle non-finite values.
Results may differ from the reference program's by a relative error of at most 0.0003.
Values sent between devices are 32-bit elements; how exact they have to be, the bound alone decides.
A program may use at most 64 MiB of HBM per device.

```python
import math
import jax
import jax.numpy as jnp
from jax import lax

TILE_SIDE = 16
G_DEV = 4096
TILES_DEV = 8
LIST = 256
CELLS = 8
TILES = 32
GAUSS = 32768


def draw_gaussians(key, part):
    keys = jax.random.split(jax.random.fold_in(key, 11), 8)
    local = jnp.arange(GAUSS, dtype=jnp.int32) % G_DEV
    home = local % TILES
    tile_x = (home % TILES_DEV).astype(jnp.float32)
    tile_y = (home // TILES_DEV).astype(jnp.float32)
    reach = 1.5 * TILE_SIDE
    centre_x = (tile_x + 0.5) * TILE_SIDE + jax.random.uniform(keys[0], (GAUSS,), jnp.float32, -reach, reach)
    centre_y = (tile_y + 0.5) * TILE_SIDE + jax.random.uniform(keys[1], (GAUSS,), jnp.float32, -reach, reach)
    depth = jax.random.uniform(keys[2], (1, GAUSS), jnp.float32, 4.0, 8.0)
    log_scales = jax.random.uniform(keys[3], (3, GAUSS), jnp.float32, 0.5, 2.5)
    quat_first = jax.random.uniform(keys[4], (1, GAUSS), jnp.float32, 1.0, 2.0)
    quat_rest = jax.random.normal(keys[5], (3, GAUSS), jnp.float32)
    logits = jax.random.uniform(keys[6], (1, GAUSS), jnp.float32, -5.0, -1.0)
    coefficients = 0.5 * jax.random.normal(keys[7], (48, GAUSS), jnp.float32)
    return jnp.concatenate([centre_x[None], centre_y[None], depth, log_scales, quat_first, quat_rest, logits, coefficients], axis=0)


def draw_tile_lists(key, part):
    per_home = G_DEV // TILES
    candidates = 25 * per_home
    rows_down = TILES // TILES_DEV
    base = jax.random.fold_in(key, 23)

    def one_list(flat):
        picked = jax.random.permutation(jax.random.fold_in(base, flat), candidates)[:LIST]
        tile_index = flat % TILES
        neighbour = picked // per_home
        member = picked % per_home
        tile_x = (tile_index % TILES_DEV + neighbour % 5 - 2) % TILES_DEV
        tile_y = (tile_index // TILES_DEV + neighbour // 5 - 2) % rows_down
        return (tile_y * TILES_DEV + tile_x + TILES * member).astype(jnp.int32)
    lists = lax.map(one_list, jnp.arange(CELLS * TILES, dtype=jnp.int32))
    return lists.reshape(CELLS, TILES, LIST)


def draw_list_blocks(key, part):
    most = LIST // 128
    blocks = jax.random.randint(jax.random.fold_in(key, 37), (CELLS, TILES), 1, most + 1)
    return blocks.at[:, 0].set(most).at[:, 1].set(1).astype(jnp.int32)


def shard_levels(own_key, dims, shards, least, largest):
    gain, own = 1.0, jax.random.fold_in(own_key, 6)
    for position, shards_of in shards:
        steps = jnp.exp(jax.random.uniform(jax.random.fold_in(own, position), (shards_of,), jnp.float32, least / len(shards), largest / len(shards)))
        gain = gain * jnp.repeat(steps, dims[position] // shards_of).reshape([-1 if axis == position else 1 for axis in range(len(dims))])
    return gain


def centred(rng, shape, spread, bound, cuts=(), kind=jnp.bfloat16):
    array = spread * jax.random.normal(rng, shape, jnp.float32)
    if cuts:
        array = array * shard_levels(rng, shape, cuts, -0.22, 0.18)
    return jnp.clip(array, -bound, bound).astype(kind)


def setup_inputs(seed: int = 0) -> dict:
    streams_of = jax.random.split(jax.random.key(seed), 7)
    return {
        "gaussians": draw_gaussians(jax.random.fold_in(streams_of[6], 71), 0),
        "tile_lists": draw_tile_lists(jax.random.fold_in(streams_of[6], 71), 0),
        "list_blocks": draw_list_blocks(jax.random.fold_in(streams_of[6], 71), 0),
        "cell_order": jax.random.permutation(streams_of[3], CELLS).astype(jnp.int32),
        "view_vector": jnp.clip(jax.random.uniform(streams_of[4], (3,), jnp.float32, 0.5, 1.0), 0.5, 1.0),
        "cotangent": centred(streams_of[5], (3, TILES, TILE_SIDE * TILE_SIDE), 1.0, 6.0, ((1, 4),), jnp.float32),
    }


BACKGROUND = 1.0
FOCAL = 6.0
BLUR = 0.3

def harmonic_basis(view_vector):
    unit_vector = view_vector / jnp.sqrt(jnp.sum(view_vector * view_vector))
    x, y, z = (unit_vector[0], unit_vector[1], unit_vector[2])
    return jnp.stack([0.28209479177387814 + 0.0 * x, -0.4886025119029199 * y, 0.4886025119029199 * z, -0.4886025119029199 * x, 1.0925484305920792 * x * y, -1.0925484305920792 * y * z, 0.31539156525252005 * (2.0 * z * z - x * x - y * y), -1.0925484305920792 * x * z, 0.5462742152960396 * (x * x - y * y), -0.5900435899266435 * y * (3.0 * x * x - y * y), 2.890611442640554 * x * y * z, -0.4570457994644658 * y * (4.0 * z * z - x * x - y * y), 0.3731763325901154 * z * (2.0 * z * z - 3.0 * x * x - 3.0 * y * y), -0.4570457994644658 * x * (4.0 * z * z - x * x - y * y), 1.445305721320277 * z * (x * x - y * y), -0.5900435899266435 * x * (x * x - 3.0 * y * y)])

def project(gaussians, harmonics):
    squared_scale = jnp.exp(2.0 * gaussians[3:6])
    quaternion = gaussians[6:10] / jnp.sqrt(lax.optimization_barrier(jnp.sum(gaussians[6:10] * gaussians[6:10], axis=0)))
    w, a, b, c = (quaternion[0], quaternion[1], quaternion[2], quaternion[3])
    row_one = (1.0 - 2.0 * (b * b + c * c), 2.0 * (a * b - w * c), 2.0 * (a * c + w * b))
    row_two = (2.0 * (a * b + w * c), 1.0 - 2.0 * (a * a + c * c), 2.0 * (b * c - w * a))
    zoom_factor = (FOCAL / gaussians[2]) ** 2
    sigma_xx = zoom_factor * sum((row_one[k] * row_one[k] * squared_scale[k] for k in range(3))) + BLUR
    sigma_xy = zoom_factor * sum((row_one[k] * row_two[k] * squared_scale[k] for k in range(3)))
    sigma_yy = zoom_factor * sum((row_two[k] * row_two[k] * squared_scale[k] for k in range(3))) + BLUR
    determinant = sigma_xx * sigma_yy - sigma_xy * sigma_xy
    opacity = jax.nn.sigmoid(gaussians[10])
    coefficients = gaussians[11:59].reshape(3, 16, -1)
    colour = 0.5 + lax.optimization_barrier(jnp.sum(coefficients * harmonics[None, :, None], axis=1))
    return jnp.stack([gaussians[0], gaussians[1], sigma_yy / determinant, -sigma_xy / determinant, sigma_xx / determinant, opacity, colour[0], colour[1], colour[2]])

def pixel_grid(tile_ids, across):
    within = jnp.arange(TILE_SIDE * TILE_SIDE, dtype=jnp.int32)
    tile_x = tile_ids % across
    tile_y = tile_ids // across
    pixel_x = (tile_x[:, None] * TILE_SIDE + within[None, :] % TILE_SIDE).astype(jnp.float32) + 0.5
    pixel_y = (tile_y[:, None] * TILE_SIDE + within[None, :] // TILE_SIDE).astype(jnp.float32) + 0.5
    return (pixel_x, pixel_y)

def render(gathered, live_mask, pixel_x, pixel_y):
    offset_x = pixel_x[:, :, None] - gathered[0][:, None, :]
    offset_y = pixel_y[:, :, None] - gathered[1][:, None, :]
    exponent = -0.5 * (gathered[2][:, None, :] * offset_x * offset_x + 2.0 * gathered[3][:, None, :] * offset_x * offset_y + gathered[4][:, None, :] * offset_y * offset_y)
    alphas = gathered[5][:, None, :] * jnp.exp(exponent) * live_mask[:, None, :]
    log_keep = jnp.log1p(-alphas)
    before_keep = jnp.cumsum(log_keep, axis=-1) - log_keep
    weights = alphas * jnp.exp(before_keep)
    colours = jnp.einsum('tpl,ctl->ctp', weights, gathered[6:9], precision=lax.Precision.HIGHEST)
    return (colours, lax.optimization_barrier(jnp.sum(log_keep, axis=-1)))

def split_blocks(gathered, live_mask, pixel_x, pixel_y, block_tiles):
    block_count = live_mask.shape[0] // block_tiles
    return (gathered.reshape(9, block_count, block_tiles, -1).transpose(1, 0, 2, 3), live_mask.reshape(block_count, block_tiles, -1), pixel_x.reshape(block_count, block_tiles, -1), pixel_y.reshape(block_count, block_tiles, -1))

def block_render(gathered, live_mask, pixel_x, pixel_y, block_tiles):
    inputs = split_blocks(gathered, live_mask, pixel_x, pixel_y, block_tiles)
    results = lax.map(lambda group: render(*group), inputs)
    width = pixel_x.shape[-1]
    return (results[0].transpose(1, 0, 2, 3).reshape(3, -1, width), results[1].reshape(-1, width))

def block_pullback(gathered, live_mask, pixel_x, pixel_y, grad_colour, keep_grad, block_tiles):
    inputs = split_blocks(gathered, live_mask, pixel_x, pixel_y, block_tiles)
    block_count = live_mask.shape[0] // block_tiles
    grad_colour = grad_colour.reshape(3, block_count, block_tiles, -1).transpose(1, 0, 2, 3)
    keep_grad = keep_grad.reshape(block_count, block_tiles, -1)

    def pull_block(group):
        values, mask, across, down, colour_part, keep_part = group
        _, pullback = jax.vjp(lambda items: render(items, mask, across, down), values)
        return pullback((colour_part, keep_part))[0]
    results = lax.map(pull_block, inputs + (grad_colour, keep_grad))
    return results.transpose(1, 0, 2, 3).reshape(9, live_mask.shape[0], -1)

def reference(gaussians, tile_lists, list_blocks, cell_order, view_vector, cotangent):
    harmonics = harmonic_basis(view_vector)
    projected = project(gaussians, harmonics).reshape(9, CELLS, G_DEV).transpose(1, 0, 2)
    tile_ids = jnp.arange(TILES, dtype=jnp.int32)
    pixel_x, pixel_y = pixel_grid(tile_ids, TILES_DEV)
    live_all = (jnp.arange(LIST, dtype=jnp.int32)[None, None, :] < 128 * list_blocks[:, :, None]).astype(jnp.float32)
    block_tiles = math.gcd(TILES_DEV, 4)

    def forward_cell(inputs):
        proj_cell, list_cell, live_cell = inputs
        return block_render(proj_cell[:, list_cell], live_cell, pixel_x, pixel_y, block_tiles)
    colours_all, keep_all = lax.map(forward_cell, (projected, tile_lists, live_all))
    positions = jnp.zeros((CELLS,), jnp.int32).at[cell_order].set(jnp.arange(CELLS, dtype=jnp.int32))
    before = (positions[None, :] < positions[:, None]).astype(jnp.float32)
    prefix = jnp.einsum('cd,dtp->ctp', before, keep_all, precision=lax.Precision.HIGHEST)
    total_keep = lax.optimization_barrier(jnp.sum(keep_all, axis=0))
    lit_prefix = jnp.exp(prefix)
    rendered = lax.optimization_barrier(jnp.sum(lit_prefix[:, None] * colours_all, axis=0)) + BACKGROUND * jnp.exp(total_keep)[None]
    grad_colour = lit_prefix[:, None] * cotangent[None]
    through = lit_prefix * lax.optimization_barrier(jnp.sum(colours_all * cotangent[None], axis=1))
    later_sum = jnp.einsum('dc,dtp->ctp', before, through, precision=lax.Precision.HIGHEST)
    keep_grad = later_sum + (BACKGROUND * jnp.exp(total_keep) * lax.optimization_barrier(jnp.sum(cotangent, axis=0)))[None]

    def backward_cell(inputs):
        proj_cell, list_cell, live_cell, colour_part, keep_part = inputs
        dgathered = block_pullback(proj_cell[:, list_cell], live_cell, pixel_x, pixel_y, colour_part, keep_part, block_tiles)
        return jnp.zeros((9, G_DEV), jnp.float32).at[:, list_cell].add(dgathered)
    dprojected = lax.map(backward_cell, (projected, tile_lists, live_all, grad_colour, keep_grad))
    dprojected = dprojected.transpose(1, 0, 2).reshape(9, -1)
    _, pullback = jax.vjp(lambda values: project(values, harmonics), gaussians)
    return (rendered, pullback(dprojected)[0])
```

```python
import functools

import jax
import jax.numpy as jnp
from jax import lax
from jax.experimental import pallas as pl
from jax.experimental.pallas import tpu as pltpu
from jax.sharding import PartitionSpec as P

TILE_SIDE = 16
LANES = 128
CHUNKS = 4
UNROLL = 4
ROWS = 16
BACKGROUND = 1.0
FOCAL = 6.0
BLUR = 0.3
F32 = jnp.float32
MESH = pl.DeviceIdType.MESH


def harmonic_basis(vx, vy, vz):
    norm = jnp.sqrt(vx * vx + vy * vy + vz * vz)
    x, y, z = vx / norm, vy / norm, vz / norm
    return [
        0.28209479177387814 + 0.0 * x,
        -0.4886025119029199 * y,
        0.4886025119029199 * z,
        -0.4886025119029199 * x,
        1.0925484305920792 * x * y,
        -1.0925484305920792 * y * z,
        0.31539156525252005 * (2.0 * z * z - x * x - y * y),
        -1.0925484305920792 * x * z,
        0.5462742152960396 * (x * x - y * y),
        -0.5900435899266435 * y * (3.0 * x * x - y * y),
        2.890611442640554 * x * y * z,
        -0.4570457994644658 * y * (4.0 * z * z - x * x - y * y),
        0.3731763325901154 * z * (2.0 * z * z - 3.0 * x * x - 3.0 * y * y),
        -0.4570457994644658 * x * (4.0 * z * z - x * x - y * y),
        1.445305721320277 * z * (x * x - y * y),
        -0.5900435899266435 * x * (x * x - 3.0 * y * y),
    ]


def conic(depth, s0, s1, s2, q0, q1, q2, q3):
    scales = [jnp.exp(2.0 * s) for s in (s0, s1, s2)]
    norm = jnp.sqrt(q0 * q0 + q1 * q1 + q2 * q2 + q3 * q3)
    w, a, b, c = q0 / norm, q1 / norm, q2 / norm, q3 / norm
    row_one = (1.0 - 2.0 * (b * b + c * c), 2.0 * (a * b - w * c), 2.0 * (a * c + w * b))
    row_two = (2.0 * (a * b + w * c), 1.0 - 2.0 * (a * a + c * c), 2.0 * (b * c - w * a))
    ratio = FOCAL / depth
    zoom = ratio * ratio
    xx = zoom * sum(row_one[k] * row_one[k] * scales[k] for k in range(3)) + BLUR
    xy = zoom * sum(row_one[k] * row_two[k] * scales[k] for k in range(3))
    yy = zoom * sum(row_two[k] * row_two[k] * scales[k] for k in range(3)) + BLUR
    det = xx * yy - xy * xy
    return yy / det, -xy / det, xx / det


def sigmoid(x):
    return 1.0 / (1.0 + jnp.exp(-x))


def pick(values, lane):
    return jnp.take_along_axis(values, lane, axis=1, mode="promise_in_bounds")


def harmonic_rows(view_ref, first, rows):
    shape = (rows, LANES)
    vx, vy, vz = (jnp.full(shape, view_ref[k], F32) for k in range(3))
    row = lax.broadcasted_iota(jnp.int32, shape, 0)
    out = jnp.zeros(shape, F32)
    for k, value in enumerate(harmonic_basis(vx, vy, vz)):
        out = jnp.where(row == first + k, value, out)
    return out


def project_all(gauss_ref, view_ref, rows_ref, table_ref, loads):
    blocks = gauss_ref.shape[1] // LANES
    weights = harmonic_rows(view_ref, 3, 24)
    for k in range(blocks):
        if k % (blocks // CHUNKS) == 0:
            loads[k // (blocks // CHUNKS)].wait()
        cols = pl.ds(k * LANES, LANES)
        for r in range(11):
            rows_ref[r, pl.ds(k, 1), :] = gauss_ref[pl.ds(r, 1), cols]
        for ch in range(3):
            start = 8 + 16 * ch
            size = min(24, gauss_ref.shape[0] - start)
            part = gauss_ref[pl.ds(start, size), cols] * weights[:size]
            table_ref[6 + ch, pl.ds(k, 1), :] = 0.5 + jnp.sum(part, axis=0, keepdims=True)
    a, b, c = conic(*[rows_ref[r] for r in range(2, 10)])
    table_ref[0] = rows_ref[0]
    table_ref[1] = rows_ref[1]
    table_ref[2] = a
    table_ref[3] = b
    table_ref[4] = c
    table_ref[5] = sigmoid(rows_ref[10])


def gather_all(lists_ref, blocks_ref, table_ref, picked_ref):
    tiles, length = lists_ref.shape[1], lists_ref.shape[2]
    shape = (tiles, LANES)
    row = lax.broadcasted_iota(jnp.int32, shape, 0)
    lane = lax.broadcasted_iota(jnp.int32, shape, 1)
    limit = jnp.zeros(shape, jnp.int32)
    for t in range(tiles):
        limit = jnp.where(row == t, blocks_ref[0, t] * LANES, limit)
    row_of_tile = lax.axis_index("tile")
    centre_x = (row * TILE_SIDE + TILE_SIDE // 2).astype(F32)
    centre_y = jnp.full(shape, row_of_tile * TILE_SIDE + TILE_SIDE // 2, jnp.int32).astype(F32)
    for part in range(length // LANES):
        cols = pl.ds(part * LANES, LANES)
        index = lists_ref[0, :, cols]
        high = index // LANES
        low = index - high * LANES
        values = [jnp.zeros(shape, F32) for _ in range(9)]
        for k in range(table_ref.shape[1]):
            hit = high == k
            for r in range(9):
                line = jnp.broadcast_to(table_ref[r, pl.ds(k, 1), :], shape)
                values[r] = jnp.where(hit, pick(line, low), values[r])
        values[0] = values[0] - centre_x
        values[1] = values[1] - centre_y
        values[5] = jnp.where(lane + part * LANES < limit, values[5], 0.0)
        for r in range(9):
            picked_ref[r, :, cols] = values[r]


def split(value):
    top = value.astype(jnp.bfloat16)
    return top, (value - top.astype(F32)).astype(jnp.bfloat16)


def dot(a, b):
    return jnp.dot(a, b, preferred_element_type=F32)


def dot_rows(a, b):
    return lax.dot_general(a, b, (((1,), (1,)), ((), ())), preferred_element_type=F32)


def dot_columns(a, b):
    return lax.dot_general(a, b, (((0,), (0,)), ((), ())), preferred_element_type=F32)


def stacked(rows):
    shape = (ROWS, rows[0].shape[1])
    line = lax.broadcasted_iota(jnp.int32, shape, 0)
    out = jnp.zeros(shape, F32)
    for n, row in enumerate(rows):
        out = jnp.where(line == n, row.astype(F32), out)
    return out.astype(jnp.bfloat16)


def halves(rows):
    pieces = [split(row) for row in rows]
    return [p[0] for p in pieces], [p[1] for p in pieces]


def triangles(tri_ref):
    shape = tri_ref.shape[1:]
    row = lax.broadcasted_iota(jnp.int32, shape, 0)
    col = lax.broadcasted_iota(jnp.int32, shape, 1)
    tri_ref[0] = jnp.where(row < col, 1.0, 0.0).astype(jnp.bfloat16)
    tri_ref[1] = jnp.where(row > col, 1.0, 0.0).astype(jnp.bfloat16)


def moment_basis(pixels):
    pixel = lax.broadcasted_iota(jnp.int32, (1, pixels), 1)
    half = 0.5 * (TILE_SIDE - 1)
    px = (pixel % TILE_SIDE).astype(F32) - half
    py = (pixel // TILE_SIDE).astype(F32) - half
    return stacked([jnp.ones_like(px), px, py, px * px, px * py, py * py])


def forward(me, picked_ref, tri_ref, ratio_ref, weight_ref, parts_ref, logs_ref, seen_ref):
    tiles, length = picked_ref.shape[1], picked_ref.shape[2]
    lines = weight_ref.shape[1] // TILE_SIDE
    half = 0.5 * (TILE_SIDE - 1)

    def one_tile(t, _):
        cx, cy, a, b, c, op, c0, c1, c2 = (picked_ref[r, pl.ds(t, 1), :] for r in range(9))
        dx = lax.broadcasted_iota(jnp.int32, (TILE_SIDE, length), 0).astype(F32) - half - cx
        square = (-0.5 * a) * dx * dx
        cross = -b * dx
        curve = -0.5 * c
        for y in range(lines):
            rows = pl.ds(y * TILE_SIDE, TILE_SIDE)
            dy = (y - half) - cy
            alpha = op * jnp.exp(square + cross * dy + curve * dy * dy)
            keep = 1.0 - alpha
            top, rest = split(jnp.log(keep))
            logs_ref[0, rows, :] = top
            logs_ref[1, rows, :] = rest
            weight_ref[t, rows, :] = alpha
            ratio_ref[t, rows, :] = alpha / keep
        upper = tri_ref[0]
        before = dot(logs_ref[0], upper) + dot(logs_ref[1], upper)
        for y in range(lines):
            rows = pl.ds(y * TILE_SIDE, TILE_SIDE)
            weight = weight_ref[t, rows, :] * jnp.exp(before[y * TILE_SIDE : (y + 1) * TILE_SIDE])
            weight_ref[t, rows, :] = weight
            top, rest = split(weight)
            parts_ref[t, 0, rows, :] = top
            parts_ref[t, 1, rows, :] = rest
        tops, rests = halves([c0, c1, c2])
        tint = stacked(tops + rests)
        colour = dot_rows(tint, parts_ref[t, 0]) + dot_rows(tint, parts_ref[t, 1])
        for ch in range(3):
            seen_ref[me, ch, pl.ds(t, 1), :] = colour[ch : ch + 1] + colour[3 + ch : 4 + ch]
        ones = jnp.ones((ROWS, length), jnp.bfloat16)
        total = dot_rows(ones, logs_ref[0]) + dot_rows(ones, logs_ref[1])
        seen_ref[me, 3, pl.ds(t, 1), :] = jnp.exp(total[:1])
        return 0

    lax.fori_loop(0, tiles, one_tile, 0, unroll=UNROLL)


def backward(picked_ref, tri_ref, ratio_ref, weight_ref, parts_ref, logs_ref, tint_ref, grads_ref):
    tiles, length = picked_ref.shape[1], picked_ref.shape[2]
    lines = weight_ref.shape[1] // TILE_SIDE
    basis = moment_basis(weight_ref.shape[1])

    def one_tile(t, _):
        cx, cy = (picked_ref[r, pl.ds(t, 1), :] for r in range(2))
        tops, rests = halves([picked_ref[6 + ch, pl.ds(t, 1), :] for ch in range(3)])
        glow, faint = halves([tint_ref[ch, pl.ds(t, 1), :] for ch in range(4)])
        light = dot_columns(stacked(glow[:3] + glow[:3] + faint[:3]), stacked(tops + rests + tops))
        ones = jnp.ones((ROWS, length), jnp.bfloat16)
        for y in range(lines):
            rows = pl.ds(y * TILE_SIDE, TILE_SIDE)
            lit = weight_ref[t, rows, :] * light[y * TILE_SIDE : (y + 1) * TILE_SIDE]
            weight_ref[t, rows, :] = lit
            top, rest = split(lit)
            logs_ref[0, rows, :] = top
            logs_ref[1, rows, :] = rest
        lower = tri_ref[1]
        later = dot(logs_ref[0], lower) + dot(logs_ref[1], lower)
        later = later + dot_columns(stacked([glow[3], faint[3]]), ones)
        for y in range(lines):
            rows = pl.ds(y * TILE_SIDE, TILE_SIDE)
            slope = weight_ref[t, rows, :] - ratio_ref[t, rows, :] * later[y * TILE_SIDE : (y + 1) * TILE_SIDE]
            top, rest = split(slope)
            logs_ref[2, rows, :] = top
            logs_ref[3, rows, :] = rest
        sums = dot(basis, logs_ref[2]) + dot(basis, logs_ref[3])
        m0, mx, my, mxx, mxy, myy = (sums[n : n + 1] for n in range(6))
        here = pl.ds(t, 1)
        grads_ref[0, here, :] = mx - cx * m0
        grads_ref[1, here, :] = my - cy * m0
        grads_ref[2, here, :] = mxx - 2.0 * cx * mx + cx * cx * m0
        grads_ref[3, here, :] = mxy - cx * my - cy * mx + cx * cy * m0
        grads_ref[4, here, :] = myy - 2.0 * cy * my + cy * cy * m0
        grads_ref[5, here, :] = m0
        tint = stacked(glow[:3] + faint[:3])
        colour = dot(tint, parts_ref[t, 0]) + dot(tint, parts_ref[t, 1])
        for ch in range(3):
            grads_ref[6 + ch, here, :] = colour[ch : ch + 1] + colour[3 + ch : 4 + ch]
        return 0

    lax.fori_loop(0, tiles, one_tile, 0, unroll=UNROLL)


def scatter_all(lists_ref, grads_ref, spread_ref, hot_ref, share_ref, blocks):
    tiles, length = grads_ref.shape[1], grads_ref.shape[2]
    for t in range(tiles):
        index = lists_ref[0, pl.ds(t, 1), :]
        high = index // LANES
        low = index - high * LANES
        cols = pl.ds(t * length, length)
        line = lax.broadcasted_iota(jnp.int32, (LANES, length), 0)
        hot_ref[:, cols] = jnp.where(line == low, 1.0, 0.0).astype(jnp.bfloat16)
        hit = lax.broadcasted_iota(jnp.int32, (blocks, length), 0) == high
        for r in range(9):
            value = grads_ref[r, pl.ds(t, 1), :]
            top = value.astype(jnp.bfloat16).astype(F32)
            rest = value - top
            rows = pl.ds(r * blocks, blocks)
            spread_ref[0, rows, cols] = jnp.where(hit, top, 0.0).astype(jnp.bfloat16)
            spread_ref[1, rows, cols] = jnp.where(hit, rest, 0.0).astype(jnp.bfloat16)
    dims = (((1,), (1,)), ((), ()))
    hot = hot_ref[...]
    total = lax.dot_general(spread_ref[0], hot, dims, preferred_element_type=F32)
    total = total + lax.dot_general(spread_ref[1], hot, dims, preferred_element_type=F32)
    shares, _, lines, _ = share_ref.shape
    for s in range(shares):
        for r in range(9):
            share_ref[s, r] = total[r * blocks + s * lines : r * blocks + (s + 1) * lines]


def pull_back(gauss_ref, view_ref, own_ref, grads, out_ref):
    lines = own_ref.shape[1]
    base = lax.axis_index("tile") * (lines * LANES)
    for k in range(lines):
        cols = pl.ds(pl.multiple_of(base + k * LANES, LANES), LANES)
        for r in range(11):
            own_ref[r, pl.ds(k, 1), :] = gauss_ref[pl.ds(r, 1), cols]
    (a, b, c), pull = jax.vjp(conic, *[own_ref[r] for r in range(2, 10)])
    opacity = sigmoid(own_ref[10])
    sx, sy, sxx, sxy, syy, s0 = grads[:6]
    rows = [a * sx + b * sy, b * sx + c * sy]
    rows += list(pull((-0.5 * sxx, -sxy, -0.5 * syy)))
    rows.append(s0 * (1.0 - opacity))
    basis = harmonic_rows(view_ref, 0, 16)
    for k in range(lines):
        cols = pl.ds(k * LANES, LANES)
        for r in range(11):
            out_ref[pl.ds(r, 1), cols] = rows[r][k : k + 1]
        for ch in range(3):
            out_ref[pl.ds(11 + 16 * ch, 16), cols] = basis * grads[6 + ch][k : k + 1]


def kernel(
    cells, shares,
    gauss_in, lists_in, blocks_in, order_in, view_in, cot_in,
    image_ref, out_ref,
    gauss_ref, lists_ref, blocks_ref, order_ref, view_ref, cot_ref, load_sem,
    rows_ref, table_ref, picked_ref, tri_ref, ratio_ref, weight_ref, parts_ref, logs_ref, tint_ref, seen_ref,
    grads_ref, spread_ref, hot_ref, share_ref, came_ref, own_ref,
    cell_send, cell_recv, tile_send, tile_recv,
):
    me = lax.axis_index("cell")
    row_of_tile = lax.axis_index("tile")
    chunk = gauss_ref.shape[1] // CHUNKS
    pairs = [(view_in, view_ref)]
    pairs += [
        (gauss_in.at[:, pl.ds(n * chunk, chunk)], gauss_ref.at[:, pl.ds(n * chunk, chunk)])
        for n in range(CHUNKS)
    ]
    pairs += [(lists_in, lists_ref), (blocks_in, blocks_ref), (cot_in, cot_ref), (order_in, order_ref)]
    loads = [pltpu.make_async_copy(src, dst, load_sem.at[n]) for n, (src, dst) in enumerate(pairs)]
    for load in loads:
        load.start()
    barrier = pltpu.get_barrier_semaphore()
    cell_peers = [lax.rem(me + off, cells) for off in range(1, cells)]
    tile_peers = [lax.rem(row_of_tile + off, shares) for off in range(1, shares)]
    for peer in cell_peers:
        pl.semaphore_signal(barrier, inc=1, device_id=(peer, row_of_tile), device_id_type=MESH)
    for peer in tile_peers:
        pl.semaphore_signal(barrier, inc=1, device_id=(me, peer), device_id_type=MESH)

    triangles(tri_ref)
    loads[0].wait()
    project_all(gauss_ref, view_ref, rows_ref, table_ref, loads[1 : 1 + CHUNKS])
    for load in loads[1 + CHUNKS :]:
        load.wait()
    gather_all(lists_ref, blocks_ref, table_ref, picked_ref)
    forward(me, picked_ref, tri_ref, ratio_ref, weight_ref, parts_ref, logs_ref, seen_ref)
    pl.semaphore_wait(barrier, cells + shares - 2)
    copies = []
    for n, peer in enumerate(cell_peers):
        copy = pltpu.make_async_remote_copy(
            src_ref=seen_ref.at[me], dst_ref=seen_ref.at[me],
            send_sem=cell_send.at[n], recv_sem=cell_recv.at[n],
            device_id=(peer, row_of_tile), device_id_type=MESH,
        )
        copy.start()
        copies.append(copy)
    for copy in copies:
        copy.wait()

    shape = seen_ref.shape[2:]
    light = [jnp.full(shape, BACKGROUND, F32) for _ in range(3)]
    behind = [jnp.zeros(shape, F32) for _ in range(3)]
    ahead = jnp.ones(shape, F32)
    passed = jnp.zeros(shape, jnp.int32)
    for s in reversed(range(cells)):
        cell = order_ref[s]
        mine = jnp.full(shape, cell, jnp.int32) == me
        kept = seen_ref[cell, 3]
        ahead = jnp.where(passed == 1, ahead * kept, ahead)
        for ch in range(3):
            behind[ch] = jnp.where(mine, light[ch], behind[ch])
            light[ch] = seen_ref[cell, ch] + kept * light[ch]
        passed = jnp.where(mine, 1, passed)
    after = jnp.zeros(shape, F32)
    for ch in range(3):
        image_ref[ch] = light[ch]
        tint = ahead * cot_ref[ch]
        tint_ref[ch] = tint
        after = after + tint * behind[ch]
    tint_ref[3] = after * seen_ref[me, 3]

    backward(picked_ref, tri_ref, ratio_ref, weight_ref, parts_ref, logs_ref, tint_ref, grads_ref)
    scatter_all(lists_ref, grads_ref, spread_ref, hot_ref, share_ref, table_ref.shape[1])
    copies = []
    for n, peer in enumerate(tile_peers):
        copy = pltpu.make_async_remote_copy(
            src_ref=share_ref.at[peer], dst_ref=came_ref.at[n],
            send_sem=tile_send.at[n], recv_sem=tile_recv.at[n],
            device_id=(me, peer), device_id_type=MESH,
        )
        copy.start()
        copies.append(copy)
    for copy in copies:
        copy.wait()
    grads = []
    for r in range(9):
        value = share_ref[row_of_tile, r]
        for n in range(shares - 1):
            value = value + came_ref[n, r]
        grads.append(value)
    pull_back(gauss_ref, view_ref, own_ref, grads, out_ref)


def finish(image_in, rows_in, image_ref, rows_ref):
    image_ref[...] = image_in[...]
    rows_ref[...] = rows_in[...]


def solution(mesh):
    cells, shares = mesh.shape["cell"], mesh.shape["tile"]

    def on_device(gaussians, tile_lists, list_blocks, cell_order, view_vector, cotangent):
        tiles, length = tile_lists.shape[1:]
        pixels = cotangent.shape[2]
        count = gaussians.shape[1]
        blocks = count // LANES
        lines = blocks // shares
        vmem = pl.BlockSpec(memory_space=pltpu.VMEM)
        image, rows = pl.pallas_call(
            functools.partial(kernel, cells, shares),
            name="splat_step",
            out_shape=(
                jax.ShapeDtypeStruct(cotangent.shape, F32),
                jax.ShapeDtypeStruct((gaussians.shape[0], count // shares), F32),
            ),
            in_specs=[pl.BlockSpec(memory_space=pl.ANY)] * 6,
            out_specs=(vmem, vmem),
            scratch_shapes=[
                pltpu.VMEM(gaussians.shape, F32),
                pltpu.VMEM(tile_lists.shape, jnp.int32),
                pltpu.SMEM(list_blocks.shape, jnp.int32),
                pltpu.SMEM(cell_order.shape, jnp.int32),
                pltpu.SMEM(view_vector.shape, F32),
                pltpu.VMEM(cotangent.shape, F32),
                pltpu.SemaphoreType.DMA((CHUNKS + 5,)),
                pltpu.VMEM((11, blocks, LANES), F32),
                pltpu.VMEM((9, blocks, LANES), F32),
                pltpu.VMEM((9, tiles, length), F32),
                pltpu.VMEM((2, length, length), jnp.bfloat16),
                pltpu.VMEM((tiles, pixels, length), F32),
                pltpu.VMEM((tiles, pixels, length), F32),
                pltpu.VMEM((tiles, 2, pixels, length), jnp.bfloat16),
                pltpu.VMEM((4, pixels, length), jnp.bfloat16),
                pltpu.VMEM((4, tiles, pixels), F32),
                pltpu.VMEM((cells, 4, tiles, pixels), F32),
                pltpu.VMEM((9, tiles, length), F32),
                pltpu.VMEM((2, 9 * blocks, tiles * length), jnp.bfloat16),
                pltpu.VMEM((LANES, tiles * length), jnp.bfloat16),
                pltpu.VMEM((shares, 9, lines, LANES), F32),
                pltpu.VMEM((shares - 1, 9, lines, LANES), F32),
                pltpu.VMEM((11, lines, LANES), F32),
                pltpu.SemaphoreType.DMA((cells - 1,)),
                pltpu.SemaphoreType.DMA((cells - 1,)),
                pltpu.SemaphoreType.DMA((shares - 1,)),
                pltpu.SemaphoreType.DMA((shares - 1,)),
            ],
            compiler_params=pltpu.CompilerParams(
                collective_id=0, has_side_effects=True, vmem_limit_bytes=24 * 1024 * 1024
            ),
        )(*[
            pltpu.with_memory_space_constraint(x, pltpu.HBM)
            for x in (gaussians, tile_lists, list_blocks, cell_order, view_vector, cotangent)
        ])
        return pl.pallas_call(
            finish,
            name="finish",
            out_shape=(
                jax.ShapeDtypeStruct(image.shape, F32),
                jax.ShapeDtypeStruct(rows.shape, F32),
            ),
            in_specs=[vmem] * 2,
            out_specs=(vmem, vmem),
            compiler_params=pltpu.CompilerParams(vmem_limit_bytes=4 * 1024 * 1024),
        )(image, rows)

    placed = (
        P(None, "cell"),
        P("cell", "tile", None),
        P("cell", "tile"),
        P(),
        P(),
        P(None, "tile", None),
    )
    return jax.shard_map(
        on_device,
        mesh=mesh,
        in_specs=placed,
        out_specs=(P(None, "tile", None), P(None, ("cell", "tile"))),
        check_vma=False,
    )
```

```python
import functools

import jax
import jax.numpy as jnp
from jax import lax
from jax.experimental import pallas as pl
from jax.experimental.pallas import tpu as pltpu
from jax.sharding import PartitionSpec as P

TILE_SIDE = 16
LANES = 128
CHUNKS = 4
UNROLL = 2
ROWS = 16
SUBLANES = 8
WIDE = 256
FORM_ROWS = 32
NOTHING = -1e9
LOG2E = 1.4426950408889634
BACKGROUND = 1.0
FOCAL = 6.0
BLUR = 0.3
F32 = jnp.float32
MESH = pl.DeviceIdType.MESH


def harmonic_basis(vx, vy, vz):
    norm = jnp.sqrt(vx * vx + vy * vy + vz * vz)
    x, y, z = vx / norm, vy / norm, vz / norm
    return [
        0.28209479177387814 + 0.0 * x,
        -0.4886025119029199 * y,
        0.4886025119029199 * z,
        -0.4886025119029199 * x,
        1.0925484305920792 * x * y,
        -1.0925484305920792 * y * z,
        0.31539156525252005 * (2.0 * z * z - x * x - y * y),
        -1.0925484305920792 * x * z,
        0.5462742152960396 * (x * x - y * y),
        -0.5900435899266435 * y * (3.0 * x * x - y * y),
        2.890611442640554 * x * y * z,
        -0.4570457994644658 * y * (4.0 * z * z - x * x - y * y),
        0.3731763325901154 * z * (2.0 * z * z - 3.0 * x * x - 3.0 * y * y),
        -0.4570457994644658 * x * (4.0 * z * z - x * x - y * y),
        1.445305721320277 * z * (x * x - y * y),
        -0.5900435899266435 * x * (x * x - 3.0 * y * y),
    ]


def conic(depth, s0, s1, s2, q0, q1, q2, q3):
    scales = [jnp.exp(2.0 * s) for s in (s0, s1, s2)]
    norm = jnp.sqrt(q0 * q0 + q1 * q1 + q2 * q2 + q3 * q3)
    w, a, b, c = q0 / norm, q1 / norm, q2 / norm, q3 / norm
    row_one = (1.0 - 2.0 * (b * b + c * c), 2.0 * (a * b - w * c), 2.0 * (a * c + w * b))
    row_two = (2.0 * (a * b + w * c), 1.0 - 2.0 * (a * a + c * c), 2.0 * (b * c - w * a))
    ratio = FOCAL / depth
    zoom = ratio * ratio
    xx = zoom * sum(row_one[k] * row_one[k] * scales[k] for k in range(3)) + BLUR
    xy = zoom * sum(row_one[k] * row_two[k] * scales[k] for k in range(3))
    yy = zoom * sum(row_two[k] * row_two[k] * scales[k] for k in range(3)) + BLUR
    det = xx * yy - xy * xy
    return yy / det, -xy / det, xx / det


def sigmoid(x):
    return 1.0 / (1.0 + jnp.exp(-x))


def pick(values, lane):
    return jnp.take_along_axis(values, lane, axis=1, mode="promise_in_bounds")


def harmonic_rows(view_ref, first, rows):
    shape = (rows, LANES)
    vx, vy, vz = (jnp.full(shape, view_ref[k], F32) for k in range(3))
    row = lax.broadcasted_iota(jnp.int32, shape, 0)
    out = jnp.zeros(shape, F32)
    for k, value in enumerate(harmonic_basis(vx, vy, vz)):
        out = jnp.where(row == first + k, value, out)
    return out


def project_all(gauss_ref, view_ref, rows_ref, table_ref, loads):
    blocks = gauss_ref.shape[1] // LANES
    weights = harmonic_rows(view_ref, 3, 24)
    for k in range(blocks):
        if k % (blocks // CHUNKS) == 0:
            loads[k // (blocks // CHUNKS)].wait()
        cols = pl.ds(k * LANES, LANES)
        for r in range(11):
            rows_ref[r, pl.ds(k, 1), :] = gauss_ref[pl.ds(r, 1), cols]
        for ch in range(3):
            start = 8 + 16 * ch
            size = min(24, gauss_ref.shape[0] - start)
            part = gauss_ref[pl.ds(start, size), cols] * weights[:size]
            table_ref[6 + ch, pl.ds(k, 1), :] = 0.5 + jnp.sum(part, axis=0, keepdims=True)
    a, b, c = conic(*[rows_ref[r] for r in range(2, 10)])
    table_ref[0] = rows_ref[0]
    table_ref[1] = rows_ref[1]
    table_ref[2] = a
    table_ref[3] = b
    table_ref[4] = c
    table_ref[5] = sigmoid(rows_ref[10])


def entry_of(part, length):
    at = lax.broadcasted_iota(jnp.int32, (SUBLANES, LANES), 1) + part * LANES
    return (at % SUBLANES) * (length // SUBLANES) + at // SUBLANES


def gather_all(lists_ref, blocks_ref, table_ref, index_ref, picked_ref):
    tiles, length = lists_ref.shape[1], lists_ref.shape[2]
    shape = (tiles, LANES)
    row = lax.broadcasted_iota(jnp.int32, shape, 0)
    limit = jnp.zeros(shape, jnp.int32)
    for t in range(tiles):
        limit = jnp.where(row == t, blocks_ref[0, t] * LANES, limit)
    row_of_tile = lax.axis_index("tile")
    centre_x = (row * TILE_SIDE + TILE_SIDE // 2).astype(F32)
    centre_y = jnp.full(shape, row_of_tile * TILE_SIDE + TILE_SIDE // 2, jnp.int32).astype(F32)
    for part in range(length // LANES):
        cols = pl.ds(part * LANES, LANES)
        entry = jnp.broadcast_to(entry_of(part, length)[:1], shape)
        index = jnp.zeros(shape, jnp.int32)
        for source in range(length // LANES):
            moved = pick(lists_ref[0, :, pl.ds(source * LANES, LANES)], entry % LANES)
            index = jnp.where(entry // LANES == source, moved, index)
        index_ref[:, cols] = index
        high = index // LANES
        low = index - high * LANES
        values = [jnp.zeros(shape, F32) for _ in range(9)]
        for k in range(table_ref.shape[1]):
            hit = high == k
            for r in range(9):
                line = jnp.broadcast_to(table_ref[r, pl.ds(k, 1), :], shape)
                values[r] = jnp.where(hit, pick(line, low), values[r])
        values[0] = values[0] - centre_x
        values[1] = values[1] - centre_y
        values[5] = jnp.where(entry < limit, values[5], 0.0)
        for r in range(9):
            picked_ref[r, :, cols] = values[r]


def split(value):
    top = value.astype(jnp.bfloat16)
    return top, (value - top.astype(F32)).astype(jnp.bfloat16)


def dot(a, b):
    return jnp.dot(a, b, preferred_element_type=F32)


def dot_rows(a, b):
    return lax.dot_general(a, b, (((1,), (1,)), ((), ())), preferred_element_type=F32)


def dot_columns(a, b):
    return lax.dot_general(a, b, (((0,), (0,)), ((), ())), preferred_element_type=F32)


def pieces(value, count):
    out = []
    for _ in range(count):
        top = value.astype(jnp.bfloat16).astype(F32)
        out.append(top)
        value = value - top
    return out


def set_rows(ref, tiles, first, values):
    for n, value in enumerate(values):
        for part in range(ref.shape[0]):
            ref[part, pl.ds((first + n) * tiles, tiles), :] = value[:, part * LANES : (part + 1) * LANES]


def rows_of(ref, t, count, tiles):
    halves = [ref.at[part][pl.ds(t, count, stride=tiles), :] for part in range(ref.shape[0])]
    return jnp.concatenate(halves, axis=1).astype(jnp.bfloat16)


def pixel_basis(basis_ref):
    shape = basis_ref.shape
    pixel = lax.broadcasted_iota(jnp.int32, shape, 1)
    row = lax.broadcasted_iota(jnp.int32, shape, 0)
    half = 0.5 * (TILE_SIDE - 1)
    px = (pixel % TILE_SIDE).astype(F32) - half
    py = (pixel // TILE_SIDE).astype(F32) - half
    out = jnp.zeros(shape, F32)
    for n, value in enumerate([jnp.ones_like(px), px, py, px * px, px * py, py * py]):
        out = jnp.where((row % 6 == n) & (row < 18), value, out)
    basis_ref[...] = out.astype(jnp.bfloat16)


def form_all(picked_ref, cot_ref, form_ref, glow_ref):
    tiles = picked_ref.shape[1]
    cx, cy, a, b, c, op = (picked_ref[r] for r in range(6))
    sx = a * cx + b * cy
    sy = b * cx + c * cy
    level = jnp.where(op > 0.0, jnp.log(jnp.maximum(op, 1e-37)), NOTHING)
    forms = [level - 0.5 * (cx * sx + cy * sy), sx, sy, -0.5 * a, -b, -0.5 * c]
    forms = [pieces(value * LOG2E, 3) for value in forms]
    for p in range(3):
        set_rows(form_ref, tiles, 6 * p, [form[p] for form in forms])
    tints = [pieces(picked_ref[6 + ch], 2) for ch in range(3)]
    for n, p in enumerate((0, 0, 1)):
        set_rows(form_ref, tiles, 18 + 3 * n, [tint[p] for tint in tints])
    set_rows(form_ref, tiles, 27, [jnp.zeros_like(cx)] * 5)
    cots = [pieces(cot_ref[ch], 2) for ch in range(3)]
    blank = jnp.zeros_like(cot_ref[0])
    set_rows(glow_ref, tiles, 0, [blank] * 18)
    for n, p in enumerate((0, 1, 0)):
        set_rows(glow_ref, tiles, 18 + 3 * n, [cot[p] for cot in cots])
    set_rows(glow_ref, tiles, 27, [blank] * 5)


def forward(me, form_ref, basis_ref, alpha_ref, weight_ref, parts_ref, crit_ref, tone_ref):
    tiles, length, pixels = alpha_ref.shape
    shape = (SUBLANES, pixels)
    line = lax.broadcasted_iota(jnp.int32, shape, 0)

    def one_tile(t, _):
        form = rows_of(form_ref, t, FORM_ROWS, tiles)
        level = dot_columns(form, basis_ref[...])
        through = jnp.ones(shape, F32)
        for v in range(length // SUBLANES):
            rows = pl.ds(v * SUBLANES, SUBLANES)
            alpha = jnp.exp2(level[v * SUBLANES : (v + 1) * SUBLANES])
            alpha_ref[t, rows, :] = alpha
            weight = alpha * through
            weight_ref[t, rows, :] = weight
            through = through - weight
        for d in (1, 2, 4):
            through = jnp.where(line >= d, through * pltpu.roll(through, d, 0), through)
        crit_ref[me, 0, pl.ds(t, 1), :] = through[SUBLANES - 1 :]
        ahead = jnp.where(line >= 1, pltpu.roll(through, 1, 0), 1.0)
        ahead = jnp.concatenate([ahead, ahead], axis=0)
        for v in range(length // ROWS):
            rows = pl.ds(v * ROWS, ROWS)
            weight = weight_ref[t, rows, :] * ahead
            weight_ref[t, rows, :] = weight
            top, rest = split(weight)
            parts_ref[t, 0, rows, :] = top
            parts_ref[t, 1, rows, :] = rest
        tint = form[FORM_ROWS - ROWS :]
        colour = dot(tint, parts_ref[t, 0]) + dot(tint, parts_ref[t, 1])
        skip = 18 - (FORM_ROWS - ROWS)
        for ch in range(3):
            tone_ref[me, ch, pl.ds(t, 1), :] = colour[skip + ch : skip + ch + 1] + colour[skip + 6 + ch : skip + 7 + ch]
        return 0

    lax.fori_loop(0, tiles, one_tile, 0, unroll=UNROLL)


def local_backward(form_ref, glow_ref, alpha_ref, weight_ref, ends_ref):
    tiles, length, pixels = alpha_ref.shape
    shape = (SUBLANES, pixels)
    line = lax.broadcasted_iota(jnp.int32, shape, 0)

    def one_tile(t, _):
        light = dot_columns(rows_of(form_ref, t, FORM_ROWS, tiles), rows_of(glow_ref, t, FORM_ROWS, tiles))
        seen = jnp.zeros(shape, F32)
        keep = jnp.ones(shape, F32)
        for v in reversed(range(length // SUBLANES)):
            rows = pl.ds(v * SUBLANES, SUBLANES)
            alpha = alpha_ref[t, rows, :]
            weight = weight_ref[t, rows, :]
            change = light[v * SUBLANES : (v + 1) * SUBLANES] - seen
            alpha_ref[t, rows, :] = weight * change
            weight_ref[t, rows, :] = weight * keep
            seen = seen + alpha * change
            keep = keep - alpha * keep
        for d in (1, 2, 4):
            inside = line < SUBLANES - d
            seen = jnp.where(inside, seen + keep * pltpu.roll(seen, SUBLANES - d, 0), seen)
            keep = jnp.where(inside, keep * pltpu.roll(keep, SUBLANES - d, 0), keep)
        inside = line < SUBLANES - 1
        ends_ref[t, 0] = jnp.where(inside, pltpu.roll(seen, SUBLANES - 1, 0), 0.0)
        ends_ref[t, 1] = jnp.where(inside, pltpu.roll(keep, SUBLANES - 1, 0), 1.0)
        return 0

    lax.fori_loop(0, tiles, one_tile, 0, unroll=UNROLL)


def mark_all(index_ref, hot_ref, hit_ref):
    tiles, length = index_ref.shape
    low_size, blocks = hot_ref.shape[0], hit_ref.shape[0]
    for t in range(tiles):
        index = index_ref[pl.ds(t, 1), :]
        high = index // low_size
        low = index - high * low_size
        cols = pl.ds(t * length, length)
        line = lax.broadcasted_iota(jnp.int32, (low_size, length), 0)
        hot_ref[:, cols] = jnp.where(line == low, 1.0, 0.0).astype(jnp.bfloat16)
        hit_ref[:, cols] = jnp.where(lax.broadcasted_iota(jnp.int32, (blocks, length), 0) == high, 1.0, 0.0)


def backward(basis_ref, alpha_ref, weight_ref, parts_ref, ends_ref, scene_ref, tint_ref, slope_ref, moments_ref):
    tiles, length, pixels = alpha_ref.shape
    basis = basis_ref[:ROWS]

    def one_tile(t, _):
        ahead = scene_ref[0, pl.ds(t, 1), :]
        behind = scene_ref[1, pl.ds(t, 1), :]
        under = ahead * (ends_ref[t, 0] + ends_ref[t, 1] * behind)
        under = jnp.concatenate([under, under], axis=0)
        for v in range(length // ROWS):
            rows = pl.ds(v * ROWS, ROWS)
            top, rest = split(ahead * alpha_ref[t, rows, :] - under * weight_ref[t, rows, :])
            slope_ref[t, 0, rows, :] = top
            slope_ref[t, 1, rows, :] = rest
        sums = dot_rows(basis, slope_ref[t, 0]) + dot_rows(basis, slope_ref[t, 1])
        tint = rows_of(tint_ref, t, ROWS, tiles)
        colour = dot_rows(tint, parts_ref[t, 0]) + dot_rows(tint, parts_ref[t, 1])
        here = pl.ds(t, 1)
        for n in range(6):
            moments_ref[n, here, :] = sums[n : n + 1]
        for ch in range(3):
            moments_ref[6 + ch, here, :] = colour[ch : ch + 1] + colour[3 + ch : 4 + ch]
        return 0

    lax.fori_loop(0, tiles, one_tile, 0, unroll=UNROLL)


def scatter_all(picked_ref, moments_ref, grads_ref, spread_ref, hot_ref, hit_ref, share_ref):
    tiles, length = moments_ref.shape[1], moments_ref.shape[2]
    blocks = hit_ref.shape[0]
    cx, cy = picked_ref[0], picked_ref[1]
    m0, mx, my, mxx, mxy, myy = (moments_ref[n] for n in range(6))
    grads_ref[0] = mx - cx * m0
    grads_ref[1] = my - cy * m0
    grads_ref[2] = mxx - 2.0 * cx * mx + cx * cx * m0
    grads_ref[3] = mxy - cx * my - cy * mx + cx * cy * m0
    grads_ref[4] = myy - 2.0 * cy * my + cy * cy * m0
    grads_ref[5] = m0
    for ch in range(3):
        grads_ref[6 + ch] = moments_ref[6 + ch]
    for t in range(tiles):
        cols = pl.ds(t * length, length)
        hit = hit_ref[:, cols]
        for r in range(9):
            top, rest = split(hit * grads_ref[r, pl.ds(t, 1), :])
            rows = pl.ds(r * blocks, blocks)
            spread_ref[0, rows, cols] = top
            spread_ref[1, rows, cols] = rest
    hot = hot_ref[...]
    total = dot_rows(spread_ref[0], hot) + dot_rows(spread_ref[1], hot)
    shares, _, lines, _ = share_ref.shape
    for s in range(shares):
        for r in range(9):
            share_ref[s, r] = total[r * blocks + s * lines : r * blocks + (s + 1) * lines]


def pull_back(gauss_ref, view_ref, own_ref, grads, out_ref):
    lines, width = own_ref.shape[1:]
    base = lax.axis_index("tile") * (lines * width)
    for k in range(lines):
        cols = pl.ds(pl.multiple_of(base + k * width, width), width)
        for r in range(11):
            own_ref[r, pl.ds(k, 1), :] = gauss_ref[pl.ds(r, 1), cols]
    (a, b, c), pull = jax.vjp(conic, *[own_ref[r] for r in range(2, 10)])
    opacity = sigmoid(own_ref[10])
    sx, sy, sxx, sxy, syy, s0 = grads[:6]
    rows = [a * sx + b * sy, b * sx + c * sy]
    rows += list(pull((-0.5 * sxx, -sxy, -0.5 * syy)))
    rows.append(s0 * (1.0 - opacity))
    basis = jnp.concatenate([harmonic_rows(view_ref, 0, 16)] * (width // LANES), axis=1)
    for k in range(lines):
        cols = pl.ds(k * width, width)
        for r in range(11):
            out_ref[pl.ds(r, 1), cols] = rows[r][k : k + 1]
        for ch in range(3):
            out_ref[pl.ds(11 + 16 * ch, 16), cols] = basis * grads[6 + ch][k : k + 1]


def kernel(
    cells, shares,
    gauss_in, lists_in, blocks_in, order_in, view_in, cot_in,
    image_ref, out_ref,
    gauss_ref, lists_ref, blocks_ref, order_ref, view_ref, cot_ref, load_sem,
    rows_ref, table_ref, index_ref, picked_ref, form_ref, glow_ref, basis_ref, alpha_ref, weight_ref, parts_ref, slope_ref,
    ends_ref, scene_ref, tint_ref, crit_ref, tone_ref, moments_ref, grads_ref, spread_ref, hot_ref, hit_ref,
    share_ref, came_ref, own_ref,
    crit_send, crit_recv, tone_send, tone_recv, tile_send, tile_recv,
):
    me = lax.axis_index("cell")
    row_of_tile = lax.axis_index("tile")
    chunk = gauss_ref.shape[1] // CHUNKS
    pairs = [(view_in, view_ref)]
    pairs += [
        (gauss_in.at[:, pl.ds(n * chunk, chunk)], gauss_ref.at[:, pl.ds(n * chunk, chunk)])
        for n in range(CHUNKS)
    ]
    pairs += [(lists_in, lists_ref), (blocks_in, blocks_ref), (cot_in, cot_ref), (order_in, order_ref)]
    loads = [pltpu.make_async_copy(src, dst, load_sem.at[n]) for n, (src, dst) in enumerate(pairs)]
    for load in loads:
        load.start()
    barrier = pltpu.get_barrier_semaphore()
    cell_peers = [lax.rem(me + off, cells) for off in range(1, cells)]
    tile_peers = [lax.rem(row_of_tile + off, shares) for off in range(1, shares)]
    for peer in cell_peers:
        pl.semaphore_signal(barrier, inc=1, device_id=(peer, row_of_tile), device_id_type=MESH)
    for peer in tile_peers:
        pl.semaphore_signal(barrier, inc=1, device_id=(me, peer), device_id_type=MESH)

    pixel_basis(basis_ref)
    loads[0].wait()
    project_all(gauss_ref, view_ref, rows_ref, table_ref, loads[1 : 1 + CHUNKS])
    for load in loads[1 + CHUNKS :]:
        load.wait()
    gather_all(lists_ref, blocks_ref, table_ref, index_ref, picked_ref)
    form_all(picked_ref, cot_ref, form_ref, glow_ref)
    forward(me, form_ref, basis_ref, alpha_ref, weight_ref, parts_ref, crit_ref, tone_ref)
    crit_ref[me, 1] = sum(cot_ref[ch] * tone_ref[me, ch] for ch in range(3))
    pl.semaphore_wait(barrier, cells + shares - 2)
    groups = []
    for ref, send, recv in ((crit_ref, crit_send, crit_recv), (tone_ref, tone_send, tone_recv)):
        copies = []
        for n, peer in enumerate(cell_peers):
            copy = pltpu.make_async_remote_copy(
                src_ref=ref.at[me], dst_ref=ref.at[me],
                send_sem=send.at[n], recv_sem=recv.at[n],
                device_id=(peer, row_of_tile), device_id_type=MESH,
            )
            copy.start()
            copies.append(copy)
        groups.append(copies)
    local_backward(form_ref, glow_ref, alpha_ref, weight_ref, ends_ref)
    mark_all(index_ref, hot_ref, hit_ref)
    for copy in groups[0]:
        copy.wait()

    shape = crit_ref.shape[2:]
    light = BACKGROUND * (cot_ref[0] + cot_ref[1] + cot_ref[2])
    behind = jnp.zeros(shape, F32)
    ahead = jnp.ones(shape, F32)
    passed = jnp.zeros(shape, jnp.int32)
    for s in reversed(range(cells)):
        cell = order_ref[s]
        mine = jnp.full(shape, cell, jnp.int32) == me
        kept = crit_ref[cell, 0]
        ahead = jnp.where(passed == 1, ahead * kept, ahead)
        behind = jnp.where(mine, light, behind)
        light = crit_ref[cell, 1] + kept * light
        passed = jnp.where(mine, 1, passed)
    scene_ref[0] = ahead
    scene_ref[1] = behind
    tints = [pieces(ahead * cot_ref[ch], 2) for ch in range(3)]
    for p in range(2):
        set_rows(tint_ref, shape[0], 3 * p, [tint[p] for tint in tints])
    set_rows(tint_ref, shape[0], 6, [jnp.zeros(shape, F32)] * (ROWS - 6))

    backward(basis_ref, alpha_ref, weight_ref, parts_ref, ends_ref, scene_ref, tint_ref, slope_ref, moments_ref)
    scatter_all(picked_ref, moments_ref, grads_ref, spread_ref, hot_ref, hit_ref, share_ref)
    copies = []
    for n, peer in enumerate(tile_peers):
        copy = pltpu.make_async_remote_copy(
            src_ref=share_ref.at[peer], dst_ref=came_ref.at[n],
            send_sem=tile_send.at[n], recv_sem=tile_recv.at[n],
            device_id=(me, peer), device_id_type=MESH,
        )
        copy.start()
        copies.append(copy)
    for copy in groups[1]:
        copy.wait()
    image = [jnp.full(shape, BACKGROUND, F32) for _ in range(3)]
    for s in reversed(range(cells)):
        cell = order_ref[s]
        kept = crit_ref[cell, 0]
        for ch in range(3):
            image[ch] = tone_ref[cell, ch] + kept * image[ch]
    for ch in range(3):
        image_ref[ch] = image[ch]
    for copy in copies:
        copy.wait()
    grads = []
    for r in range(9):
        value = share_ref[row_of_tile, r]
        for n in range(shares - 1):
            value = value + came_ref[n, r]
        grads.append(value)
    pull_back(gauss_ref, view_ref, own_ref, grads, out_ref)


def finish(image_in, rows_in, image_ref, rows_ref):
    image_ref[...] = image_in[...]
    rows_ref[...] = rows_in[...]


def solution(mesh):
    cells, shares = mesh.shape["cell"], mesh.shape["tile"]

    def on_device(gaussians, tile_lists, list_blocks, cell_order, view_vector, cotangent):
        tiles, length = tile_lists.shape[1:]
        pixels = cotangent.shape[2]
        count = gaussians.shape[1]
        blocks = count // LANES
        groups = count // WIDE
        lines = groups // shares
        vmem = pl.BlockSpec(memory_space=pltpu.VMEM)
        image, rows = pl.pallas_call(
            functools.partial(kernel, cells, shares),
            name="splat_step",
            out_shape=(
                jax.ShapeDtypeStruct(cotangent.shape, F32),
                jax.ShapeDtypeStruct((gaussians.shape[0], count // shares), F32),
            ),
            in_specs=[pl.BlockSpec(memory_space=pl.ANY)] * 6,
            out_specs=(vmem, vmem),
            scratch_shapes=[
                pltpu.VMEM(gaussians.shape, F32),
                pltpu.VMEM(tile_lists.shape, jnp.int32),
                pltpu.SMEM(list_blocks.shape, jnp.int32),
                pltpu.SMEM(cell_order.shape, jnp.int32),
                pltpu.SMEM(view_vector.shape, F32),
                pltpu.VMEM(cotangent.shape, F32),
                pltpu.SemaphoreType.DMA((CHUNKS + 5,)),
                pltpu.VMEM((11, blocks, LANES), F32),
                pltpu.VMEM((9, blocks, LANES), F32),
                pltpu.VMEM((tiles, length), jnp.int32),
                pltpu.VMEM((9, tiles, length), F32),
                pltpu.VMEM((length // LANES, FORM_ROWS * tiles, LANES), F32),
                pltpu.VMEM((pixels // LANES, FORM_ROWS * tiles, LANES), F32),
                pltpu.VMEM((FORM_ROWS, pixels), jnp.bfloat16),
                pltpu.VMEM((tiles, length, pixels), F32),
                pltpu.VMEM((tiles, length, pixels), F32),
                pltpu.VMEM((tiles, 2, length, pixels), jnp.bfloat16),
                pltpu.VMEM((tiles, 2, length, pixels), jnp.bfloat16),
                pltpu.VMEM((tiles, 2, SUBLANES, pixels), F32),
                pltpu.VMEM((2, tiles, pixels), F32),
                pltpu.VMEM((pixels // LANES, ROWS * tiles, LANES), F32),
                pltpu.VMEM((cells, 2, tiles, pixels), F32),
                pltpu.VMEM((cells, 3, tiles, pixels), F32),
                pltpu.VMEM((9, tiles, length), F32),
                pltpu.VMEM((9, tiles, length), F32),
                pltpu.VMEM((2, 9 * groups, tiles * length), jnp.bfloat16),
                pltpu.VMEM((WIDE, tiles * length), jnp.bfloat16),
                pltpu.VMEM((groups, tiles * length), F32),
                pltpu.VMEM((shares, 9, lines, WIDE), F32),
                pltpu.VMEM((shares - 1, 9, lines, WIDE), F32),
                pltpu.VMEM((11, lines, WIDE), F32),
                pltpu.SemaphoreType.DMA((cells - 1,)),
                pltpu.SemaphoreType.DMA((cells - 1,)),
                pltpu.SemaphoreType.DMA((cells - 1,)),
                pltpu.SemaphoreType.DMA((cells - 1,)),
                pltpu.SemaphoreType.DMA((shares - 1,)),
                pltpu.SemaphoreType.DMA((shares - 1,)),
            ],
            compiler_params=pltpu.CompilerParams(
                collective_id=0, has_side_effects=True, vmem_limit_bytes=24 * 1024 * 1024
            ),
        )(*[
            pltpu.with_memory_space_constraint(x, pltpu.HBM)
            for x in (gaussians, tile_lists, list_blocks, cell_order, view_vector, cotangent)
        ])
        return pl.pallas_call(
            finish,
            name="finish",
            out_shape=(
                jax.ShapeDtypeStruct(image.shape, F32),
                jax.ShapeDtypeStruct(rows.shape, F32),
            ),
            in_specs=[vmem] * 2,
            out_specs=(vmem, vmem),
            compiler_params=pltpu.CompilerParams(vmem_limit_bytes=4 * 1024 * 1024),
        )(image, rows)

    placed = (
        P(None, "cell"),
        P("cell", "tile", None),
        P("cell", "tile"),
        P(),
        P(),
        P(None, "tile", None),
    )
    return jax.shard_map(
        on_device,
        mesh=mesh,
        in_specs=placed,
        out_specs=(P(None, "tile", None), P(None, ("cell", "tile"))),
        check_vma=False,
    )
```

```python
import functools

import jax
import jax.numpy as jnp
from jax import lax
from jax.experimental import pallas as pl
from jax.experimental.pallas import tpu as pltpu
from jax.sharding import PartitionSpec as P

TILE_SIDE = 16
LANES = 128
CHUNKS = 4
UNROLL = 8
ROWS = 16
SUBLANES = 8
WIDE = 256
FORM_ROWS = 32
NOTHING = -1e9
LOG2E = 1.4426950408889634
BACKGROUND = 1.0
FOCAL = 6.0
BLUR = 0.3
F32 = jnp.float32
MESH = pl.DeviceIdType.MESH


def harmonic_basis(vx, vy, vz):
    norm = jnp.sqrt(vx * vx + vy * vy + vz * vz)
    x, y, z = vx / norm, vy / norm, vz / norm
    return [
        0.28209479177387814 + 0.0 * x,
        -0.4886025119029199 * y,
        0.4886025119029199 * z,
        -0.4886025119029199 * x,
        1.0925484305920792 * x * y,
        -1.0925484305920792 * y * z,
        0.31539156525252005 * (2.0 * z * z - x * x - y * y),
        -1.0925484305920792 * x * z,
        0.5462742152960396 * (x * x - y * y),
        -0.5900435899266435 * y * (3.0 * x * x - y * y),
        2.890611442640554 * x * y * z,
        -0.4570457994644658 * y * (4.0 * z * z - x * x - y * y),
        0.3731763325901154 * z * (2.0 * z * z - 3.0 * x * x - 3.0 * y * y),
        -0.4570457994644658 * x * (4.0 * z * z - x * x - y * y),
        1.445305721320277 * z * (x * x - y * y),
        -0.5900435899266435 * x * (x * x - 3.0 * y * y),
    ]


def conic(depth, s0, s1, s2, q0, q1, q2, q3):
    scales = [jnp.exp(2.0 * s) for s in (s0, s1, s2)]
    norm = jnp.sqrt(q0 * q0 + q1 * q1 + q2 * q2 + q3 * q3)
    w, a, b, c = q0 / norm, q1 / norm, q2 / norm, q3 / norm
    row_one = (1.0 - 2.0 * (b * b + c * c), 2.0 * (a * b - w * c), 2.0 * (a * c + w * b))
    row_two = (2.0 * (a * b + w * c), 1.0 - 2.0 * (a * a + c * c), 2.0 * (b * c - w * a))
    ratio = FOCAL / depth
    zoom = ratio * ratio
    xx = zoom * sum(row_one[k] * row_one[k] * scales[k] for k in range(3)) + BLUR
    xy = zoom * sum(row_one[k] * row_two[k] * scales[k] for k in range(3))
    yy = zoom * sum(row_two[k] * row_two[k] * scales[k] for k in range(3)) + BLUR
    det = xx * yy - xy * xy
    return yy / det, -xy / det, xx / det


def sigmoid(x):
    return 1.0 / (1.0 + jnp.exp(-x))


def pick(values, lane):
    return jnp.take_along_axis(values, lane, axis=1, mode="promise_in_bounds")


def harmonic_rows(view_ref, first, rows):
    shape = (rows, LANES)
    vx, vy, vz = (jnp.full(shape, view_ref[k], F32) for k in range(3))
    row = lax.broadcasted_iota(jnp.int32, shape, 0)
    out = jnp.zeros(shape, F32)
    for k, value in enumerate(harmonic_basis(vx, vy, vz)):
        out = jnp.where(row == first + k, value, out)
    return out


def project_all(gauss_ref, view_ref, rows_ref, table_ref, loads):
    blocks = gauss_ref.shape[1] // LANES
    weights = harmonic_rows(view_ref, 3, 24)
    for k in range(blocks):
        if k % (blocks // CHUNKS) == 0:
            loads[k // (blocks // CHUNKS)].wait()
        cols = pl.ds(k * LANES, LANES)
        for r in range(11):
            rows_ref[r, pl.ds(k, 1), :] = gauss_ref[pl.ds(r, 1), cols]
        for ch in range(3):
            start = 8 + 16 * ch
            size = min(24, gauss_ref.shape[0] - start)
            part = gauss_ref[pl.ds(start, size), cols] * weights[:size]
            table_ref[6 + ch, pl.ds(k, 1), :] = 0.5 + jnp.sum(part, axis=0, keepdims=True)
    a, b, c = conic(*[rows_ref[r] for r in range(2, 10)])
    table_ref[0] = rows_ref[0]
    table_ref[1] = rows_ref[1]
    table_ref[2] = a
    table_ref[3] = b
    table_ref[4] = c
    table_ref[5] = sigmoid(rows_ref[10])


def entry_of(part, length):
    at = lax.broadcasted_iota(jnp.int32, (SUBLANES, LANES), 1) + part * LANES
    return (at % SUBLANES) * (length // SUBLANES) + at // SUBLANES


def gather_all(lists_ref, blocks_ref, table_ref, index_ref, picked_ref):
    tiles, length = lists_ref.shape[1], lists_ref.shape[2]
    shape = (tiles, LANES)
    row = lax.broadcasted_iota(jnp.int32, shape, 0)
    limit = jnp.zeros(shape, jnp.int32)
    for t in range(tiles):
        limit = jnp.where(row == t, blocks_ref[0, t] * LANES, limit)
    row_of_tile = lax.axis_index("tile")
    centre_x = (row * TILE_SIDE + TILE_SIDE // 2).astype(F32)
    centre_y = jnp.full(shape, row_of_tile * TILE_SIDE + TILE_SIDE // 2, jnp.int32).astype(F32)
    for part in range(length // LANES):
        cols = pl.ds(part * LANES, LANES)
        entry = jnp.broadcast_to(entry_of(part, length)[:1], shape)
        index = jnp.zeros(shape, jnp.int32)
        for source in range(length // LANES):
            moved = pick(lists_ref[0, :, pl.ds(source * LANES, LANES)], entry % LANES)
            index = jnp.where(entry // LANES == source, moved, index)
        index_ref[:, cols] = index
        high = index // LANES
        low = index - high * LANES
        values = [jnp.zeros(shape, F32) for _ in range(9)]
        for k in range(table_ref.shape[1]):
            hit = high == k
            for r in range(9):
                line = jnp.broadcast_to(table_ref[r, pl.ds(k, 1), :], shape)
                values[r] = jnp.where(hit, pick(line, low), values[r])
        values[0] = values[0] - centre_x
        values[1] = values[1] - centre_y
        values[5] = jnp.where(entry < limit, values[5], 0.0)
        for r in range(9):
            picked_ref[r, :, cols] = values[r]


def split(value):
    top = value.astype(jnp.bfloat16)
    return top, (value - top.astype(F32)).astype(jnp.bfloat16)


def dot(a, b):
    return jnp.dot(a, b, preferred_element_type=F32)


def dot_rows(a, b):
    return lax.dot_general(a, b, (((1,), (1,)), ((), ())), preferred_element_type=F32)


def dot_columns(a, b):
    return lax.dot_general(a, b, (((0,), (0,)), ((), ())), preferred_element_type=F32)


def pieces(value, count):
    out = []
    for _ in range(count):
        top = value.astype(jnp.bfloat16).astype(F32)
        out.append(top)
        value = value - top
    return out


def set_rows(ref, tiles, first, values):
    for n, value in enumerate(values):
        for part in range(ref.shape[0]):
            ref[part, pl.ds((first + n) * tiles, tiles), :] = value[:, part * LANES : (part + 1) * LANES]


def rows_of(ref, t, count, tiles):
    halves = [ref.at[part][pl.ds(t, count, stride=tiles), :] for part in range(ref.shape[0])]
    return jnp.concatenate(halves, axis=1).astype(jnp.bfloat16)


def pixel_basis(basis_ref):
    shape = basis_ref.shape
    pixel = lax.broadcasted_iota(jnp.int32, shape, 1)
    row = lax.broadcasted_iota(jnp.int32, shape, 0)
    half = 0.5 * (TILE_SIDE - 1)
    px = (pixel % TILE_SIDE).astype(F32) - half
    py = (pixel // TILE_SIDE).astype(F32) - half
    out = jnp.zeros(shape, F32)
    for n, value in enumerate([jnp.ones_like(px), px, py, px * px, px * py, py * py]):
        out = jnp.where((row % 6 == n) & (row < 18), value, out)
    basis_ref[...] = out.astype(jnp.bfloat16)


def form_all(picked_ref, cot_ref, form_ref, glow_ref):
    tiles = picked_ref.shape[1]
    cx, cy, a, b, c, op = (picked_ref[r] for r in range(6))
    sx = a * cx + b * cy
    sy = b * cx + c * cy
    level = jnp.where(op > 0.0, jnp.log(jnp.maximum(op, 1e-37)), NOTHING)
    forms = [level - 0.5 * (cx * sx + cy * sy), sx, sy, -0.5 * a, -b, -0.5 * c]
    forms = [pieces(value * LOG2E, 3) for value in forms]
    for p in range(3):
        set_rows(form_ref, tiles, 6 * p, [form[p] for form in forms])
    tints = [pieces(picked_ref[6 + ch], 2) for ch in range(3)]
    for n, p in enumerate((0, 0, 1)):
        set_rows(form_ref, tiles, 18 + 3 * n, [tint[p] for tint in tints])
    set_rows(form_ref, tiles, 27, [jnp.zeros_like(cx)] * 5)
    cots = [pieces(cot_ref[ch], 2) for ch in range(3)]
    blank = jnp.zeros_like(cot_ref[0])
    set_rows(glow_ref, tiles, 0, [blank] * 18)
    for n, p in enumerate((0, 1, 0)):
        set_rows(glow_ref, tiles, 18 + 3 * n, [cot[p] for cot in cots])
    set_rows(glow_ref, tiles, 27, [blank] * 5)


def forward(me, form_ref, basis_ref, alpha_ref, weight_ref, parts_ref, crit_ref, tone_ref):
    tiles, length, pixels = alpha_ref.shape
    shape = (SUBLANES, pixels)
    line = lax.broadcasted_iota(jnp.int32, shape, 0)

    def one_tile(t, _):
        form = rows_of(form_ref, t, FORM_ROWS, tiles)
        alpha_ref[t] = jnp.exp2(dot_columns(form, basis_ref[...]))
        through = jnp.ones(shape, F32)
        for v in range(length // SUBLANES):
            rows = pl.ds(v * SUBLANES, SUBLANES)
            weight = alpha_ref[t, rows, :] * through
            weight_ref[t, rows, :] = weight
            through = through - weight
        for d in (1, 2, 4):
            through = jnp.where(line >= d, through * pltpu.roll(through, d, 0), through)
        crit_ref[me, 0, pl.ds(t, 1), :] = through[SUBLANES - 1 :]
        ahead = jnp.where(line >= 1, pltpu.roll(through, 1, 0), 1.0)
        ahead = jnp.concatenate([ahead, ahead], axis=0)
        for v in range(length // ROWS):
            rows = pl.ds(v * ROWS, ROWS)
            weight = weight_ref[t, rows, :] * ahead
            weight_ref[t, rows, :] = weight
            top, rest = split(weight)
            parts_ref[t, 0, rows, :] = top
            parts_ref[t, 1, rows, :] = rest
        tint = form[FORM_ROWS - ROWS :]
        colour = dot(tint, parts_ref[t, 0]) + dot(tint, parts_ref[t, 1])
        skip = 18 - (FORM_ROWS - ROWS)
        for ch in range(3):
            tone_ref[me, ch, pl.ds(t, 1), :] = colour[skip + ch : skip + ch + 1] + colour[skip + 6 + ch : skip + 7 + ch]
        return 0

    lax.fori_loop(0, tiles, one_tile, 0, unroll=UNROLL)


def local_backward(form_ref, glow_ref, alpha_ref, weight_ref, ends_ref):
    tiles, length, pixels = alpha_ref.shape
    shape = (SUBLANES, pixels)
    line = lax.broadcasted_iota(jnp.int32, shape, 0)

    def one_tile(t, _):
        light = dot_columns(rows_of(form_ref, t, FORM_ROWS, tiles), rows_of(glow_ref, t, FORM_ROWS, tiles))
        seen = jnp.zeros(shape, F32)
        keep = jnp.ones(shape, F32)
        for v in reversed(range(length // SUBLANES)):
            rows = pl.ds(v * SUBLANES, SUBLANES)
            alpha = alpha_ref[t, rows, :]
            weight = weight_ref[t, rows, :]
            change = light[v * SUBLANES : (v + 1) * SUBLANES] - seen
            alpha_ref[t, rows, :] = weight * change
            weight_ref[t, rows, :] = weight * keep
            seen = seen + alpha * change
            keep = keep - alpha * keep
        for d in (1, 2, 4):
            inside = line < SUBLANES - d
            seen = jnp.where(inside, seen + keep * pltpu.roll(seen, SUBLANES - d, 0), seen)
            keep = jnp.where(inside, keep * pltpu.roll(keep, SUBLANES - d, 0), keep)
        inside = line < SUBLANES - 1
        ends_ref[t, 0] = jnp.where(inside, pltpu.roll(seen, SUBLANES - 1, 0), 0.0)
        ends_ref[t, 1] = jnp.where(inside, pltpu.roll(keep, SUBLANES - 1, 0), 1.0)
        return 0

    lax.fori_loop(0, tiles, one_tile, 0, unroll=UNROLL)


def mark_all(index_ref, hot_ref, hit_ref):
    tiles, length = index_ref.shape
    low_size, blocks = hot_ref.shape[0], hit_ref.shape[0]
    for t in range(tiles):
        index = index_ref[pl.ds(t, 1), :]
        high = index // low_size
        low = index - high * low_size
        cols = pl.ds(t * length, length)
        line = lax.broadcasted_iota(jnp.int32, (low_size, length), 0)
        hot_ref[:, cols] = jnp.where(line == low, 1.0, 0.0).astype(jnp.bfloat16)
        hit_ref[:, cols] = jnp.where(lax.broadcasted_iota(jnp.int32, (blocks, length), 0) == high, 1.0, 0.0)


def backward(basis_ref, alpha_ref, weight_ref, parts_ref, ends_ref, scene_ref, tint_ref, slope_ref, moments_ref):
    tiles, length, pixels = alpha_ref.shape
    basis = basis_ref[:ROWS]

    def one_tile(t, _):
        ahead = scene_ref[0, pl.ds(t, 1), :]
        behind = scene_ref[1, pl.ds(t, 1), :]
        under = ahead * (ends_ref[t, 0] + ends_ref[t, 1] * behind)
        under = jnp.concatenate([under, under], axis=0)
        for v in range(length // ROWS):
            rows = pl.ds(v * ROWS, ROWS)
            top, rest = split(ahead * alpha_ref[t, rows, :] - under * weight_ref[t, rows, :])
            slope_ref[t, 0, rows, :] = top
            slope_ref[t, 1, rows, :] = rest
        sums = dot_rows(basis, slope_ref[t, 0]) + dot_rows(basis, slope_ref[t, 1])
        tint = rows_of(tint_ref, t, ROWS, tiles)
        colour = dot_rows(tint, parts_ref[t, 0]) + dot_rows(tint, parts_ref[t, 1])
        here = pl.ds(t, 1)
        for n in range(6):
            moments_ref[n, here, :] = sums[n : n + 1]
        for ch in range(3):
            moments_ref[6 + ch, here, :] = colour[ch : ch + 1] + colour[3 + ch : 4 + ch]
        return 0

    lax.fori_loop(0, tiles, one_tile, 0, unroll=UNROLL)


def scatter_all(picked_ref, moments_ref, grads_ref, spread_ref, hot_ref, hit_ref, share_ref):
    tiles, length = moments_ref.shape[1], moments_ref.shape[2]
    blocks = hit_ref.shape[0]
    cx, cy = picked_ref[0], picked_ref[1]
    m0, mx, my, mxx, mxy, myy = (moments_ref[n] for n in range(6))
    grads_ref[0] = mx - cx * m0
    grads_ref[1] = my - cy * m0
    grads_ref[2] = mxx - 2.0 * cx * mx + cx * cx * m0
    grads_ref[3] = mxy - cx * my - cy * mx + cx * cy * m0
    grads_ref[4] = myy - 2.0 * cy * my + cy * cy * m0
    grads_ref[5] = m0
    for ch in range(3):
        grads_ref[6 + ch] = moments_ref[6 + ch]
    for t in range(tiles):
        cols = pl.ds(t * length, length)
        hit = hit_ref[:, cols]
        for r in range(9):
            top, rest = split(hit * grads_ref[r, pl.ds(t, 1), :])
            rows = pl.ds(r * blocks, blocks)
            spread_ref[rows, cols] = top
            spread_ref[pl.ds((9 + r) * blocks, blocks), cols] = rest
    hot = hot_ref[...]
    total = dot_rows(spread_ref[...], hot)
    total = total[: 9 * blocks] + total[9 * blocks :]
    shares, _, lines, _ = share_ref.shape
    for s in range(shares):
        for r in range(9):
            share_ref[s, r] = total[r * blocks + s * lines : r * blocks + (s + 1) * lines]


def pull_back(gauss_ref, view_ref, own_ref, grads, out_ref):
    lines, width = own_ref.shape[1:]
    base = lax.axis_index("tile") * (lines * width)
    for k in range(lines):
        cols = pl.ds(pl.multiple_of(base + k * width, width), width)
        for r in range(11):
            own_ref[r, pl.ds(k, 1), :] = gauss_ref[pl.ds(r, 1), cols]
    (a, b, c), pull = jax.vjp(conic, *[own_ref[r] for r in range(2, 10)])
    opacity = sigmoid(own_ref[10])
    sx, sy, sxx, sxy, syy, s0 = grads[:6]
    rows = [a * sx + b * sy, b * sx + c * sy]
    rows += list(pull((-0.5 * sxx, -sxy, -0.5 * syy)))
    rows.append(s0 * (1.0 - opacity))
    basis = jnp.concatenate([harmonic_rows(view_ref, 0, 16)] * (width // LANES), axis=1)
    for k in range(lines):
        cols = pl.ds(k * width, width)
        for r in range(11):
            out_ref[pl.ds(r, 1), cols] = rows[r][k : k + 1]
        for ch in range(3):
            out_ref[pl.ds(11 + 16 * ch, 16), cols] = basis * grads[6 + ch][k : k + 1]


def kernel(
    cells, shares,
    gauss_in, lists_in, blocks_in, order_in, view_in, cot_in,
    image_ref, out_ref,
    gauss_ref, lists_ref, blocks_ref, order_ref, view_ref, cot_ref, load_sem,
    rows_ref, table_ref, index_ref, picked_ref, form_ref, glow_ref, basis_ref, alpha_ref, weight_ref, parts_ref, slope_ref,
    ends_ref, scene_ref, tint_ref, crit_ref, tone_ref, moments_ref, grads_ref, spread_ref, hot_ref, hit_ref,
    share_ref, came_ref, own_ref,
    crit_send, crit_recv, tone_send, tone_recv, tile_send, tile_recv,
):
    me = lax.axis_index("cell")
    row_of_tile = lax.axis_index("tile")
    chunk = gauss_ref.shape[1] // CHUNKS
    pairs = [(view_in, view_ref)]
    pairs += [
        (gauss_in.at[:, pl.ds(n * chunk, chunk)], gauss_ref.at[:, pl.ds(n * chunk, chunk)])
        for n in range(CHUNKS)
    ]
    pairs += [(lists_in, lists_ref), (blocks_in, blocks_ref), (cot_in, cot_ref), (order_in, order_ref)]
    loads = [pltpu.make_async_copy(src, dst, load_sem.at[n]) for n, (src, dst) in enumerate(pairs)]
    for load in loads:
        load.start()
    barrier = pltpu.get_barrier_semaphore()
    cell_peers = [lax.rem(me + off, cells) for off in range(1, cells)]
    tile_peers = [lax.rem(row_of_tile + off, shares) for off in range(1, shares)]
    for peer in cell_peers:
        pl.semaphore_signal(barrier, inc=1, device_id=(peer, row_of_tile), device_id_type=MESH)
    for peer in tile_peers:
        pl.semaphore_signal(barrier, inc=1, device_id=(me, peer), device_id_type=MESH)

    pixel_basis(basis_ref)
    loads[0].wait()
    project_all(gauss_ref, view_ref, rows_ref, table_ref, loads[1 : 1 + CHUNKS])
    for load in loads[1 + CHUNKS :]:
        load.wait()
    gather_all(lists_ref, blocks_ref, table_ref, index_ref, picked_ref)
    form_all(picked_ref, cot_ref, form_ref, glow_ref)
    forward(me, form_ref, basis_ref, alpha_ref, weight_ref, parts_ref, crit_ref, tone_ref)
    crit_ref[me, 1] = sum(cot_ref[ch] * tone_ref[me, ch] for ch in range(3))
    pl.semaphore_wait(barrier, cells + shares - 2)
    groups = []
    for ref, send, recv in ((crit_ref, crit_send, crit_recv), (tone_ref, tone_send, tone_recv)):
        copies = []
        for n, peer in enumerate(cell_peers):
            copy = pltpu.make_async_remote_copy(
                src_ref=ref.at[me], dst_ref=ref.at[me],
                send_sem=send.at[n], recv_sem=recv.at[n],
                device_id=(peer, row_of_tile), device_id_type=MESH,
            )
            copy.start()
            copies.append(copy)
        groups.append(copies)
    local_backward(form_ref, glow_ref, alpha_ref, weight_ref, ends_ref)
    mark_all(index_ref, hot_ref, hit_ref)
    for copy in groups[0]:
        copy.wait()

    shape = crit_ref.shape[2:]
    light = BACKGROUND * (cot_ref[0] + cot_ref[1] + cot_ref[2])
    behind = jnp.zeros(shape, F32)
    ahead = jnp.ones(shape, F32)
    passed = jnp.zeros(shape, jnp.int32)
    for s in reversed(range(cells)):
        cell = order_ref[s]
        mine = jnp.full(shape, cell, jnp.int32) == me
        kept = crit_ref[cell, 0]
        ahead = jnp.where(passed == 1, ahead * kept, ahead)
        behind = jnp.where(mine, light, behind)
        light = crit_ref[cell, 1] + kept * light
        passed = jnp.where(mine, 1, passed)
    scene_ref[0] = ahead
    scene_ref[1] = behind
    tints = [pieces(ahead * cot_ref[ch], 2) for ch in range(3)]
    for p in range(2):
        set_rows(tint_ref, shape[0], 3 * p, [tint[p] for tint in tints])
    set_rows(tint_ref, shape[0], 6, [jnp.zeros(shape, F32)] * (ROWS - 6))

    backward(basis_ref, alpha_ref, weight_ref, parts_ref, ends_ref, scene_ref, tint_ref, slope_ref, moments_ref)
    scatter_all(picked_ref, moments_ref, grads_ref, spread_ref, hot_ref, hit_ref, share_ref)
    copies = []
    for n, peer in enumerate(tile_peers):
        copy = pltpu.make_async_remote_copy(
            src_ref=share_ref.at[peer], dst_ref=came_ref.at[n],
            send_sem=tile_send.at[n], recv_sem=tile_recv.at[n],
            device_id=(me, peer), device_id_type=MESH,
        )
        copy.start()
        copies.append(copy)
    for copy in groups[1]:
        copy.wait()
    image = [jnp.full(shape, BACKGROUND, F32) for _ in range(3)]
    for s in reversed(range(cells)):
        cell = order_ref[s]
        kept = crit_ref[cell, 0]
        for ch in range(3):
            image[ch] = tone_ref[cell, ch] + kept * image[ch]
    for ch in range(3):
        image_ref[ch] = image[ch]
    for copy in copies:
        copy.wait()
    grads = []
    for r in range(9):
        value = share_ref[row_of_tile, r]
        for n in range(shares - 1):
            value = value + came_ref[n, r]
        grads.append(value)
    pull_back(gauss_ref, view_ref, own_ref, grads, out_ref)


def finish(image_in, rows_in, image_ref, rows_ref):
    image_ref[...] = image_in[...]
    rows_ref[...] = rows_in[...]


def solution(mesh):
    cells, shares = mesh.shape["cell"], mesh.shape["tile"]

    def on_device(gaussians, tile_lists, list_blocks, cell_order, view_vector, cotangent):
        tiles, length = tile_lists.shape[1:]
        pixels = cotangent.shape[2]
        count = gaussians.shape[1]
        blocks = count // LANES
        groups = count // WIDE
        lines = groups // shares
        vmem = pl.BlockSpec(memory_space=pltpu.VMEM)
        image, rows = pl.pallas_call(
            functools.partial(kernel, cells, shares),
            name="splat_step",
            out_shape=(
                jax.ShapeDtypeStruct(cotangent.shape, F32),
                jax.ShapeDtypeStruct((gaussians.shape[0], count // shares), F32),
            ),
            in_specs=[pl.BlockSpec(memory_space=pl.ANY)] * 6,
            out_specs=(vmem, vmem),
            scratch_shapes=[
                pltpu.VMEM(gaussians.shape, F32),
                pltpu.VMEM(tile_lists.shape, jnp.int32),
                pltpu.SMEM(list_blocks.shape, jnp.int32),
                pltpu.SMEM(cell_order.shape, jnp.int32),
                pltpu.SMEM(view_vector.shape, F32),
                pltpu.VMEM(cotangent.shape, F32),
                pltpu.SemaphoreType.DMA((CHUNKS + 5,)),
                pltpu.VMEM((11, blocks, LANES), F32),
                pltpu.VMEM((9, blocks, LANES), F32),
                pltpu.VMEM((tiles, length), jnp.int32),
                pltpu.VMEM((9, tiles, length), F32),
                pltpu.VMEM((length // LANES, FORM_ROWS * tiles, LANES), F32),
                pltpu.VMEM((pixels // LANES, FORM_ROWS * tiles, LANES), F32),
                pltpu.VMEM((FORM_ROWS, pixels), jnp.bfloat16),
                pltpu.VMEM((tiles, length, pixels), F32),
                pltpu.VMEM((tiles, length, pixels), F32),
                pltpu.VMEM((tiles, 2, length, pixels), jnp.bfloat16),
                pltpu.VMEM((tiles, 2, length, pixels), jnp.bfloat16),
                pltpu.VMEM((tiles, 2, SUBLANES, pixels), F32),
                pltpu.VMEM((2, tiles, pixels), F32),
                pltpu.VMEM((pixels // LANES, ROWS * tiles, LANES), F32),
                pltpu.VMEM((cells, 2, tiles, pixels), F32),
                pltpu.VMEM((cells, 3, tiles, pixels), F32),
                pltpu.VMEM((9, tiles, length), F32),
                pltpu.VMEM((9, tiles, length), F32),
                pltpu.VMEM((18 * groups, tiles * length), jnp.bfloat16),
                pltpu.VMEM((WIDE, tiles * length), jnp.bfloat16),
                pltpu.VMEM((groups, tiles * length), F32),
                pltpu.VMEM((shares, 9, lines, WIDE), F32),
                pltpu.VMEM((shares - 1, 9, lines, WIDE), F32),
                pltpu.VMEM((11, lines, WIDE), F32),
                pltpu.SemaphoreType.DMA((cells - 1,)),
                pltpu.SemaphoreType.DMA((cells - 1,)),
                pltpu.SemaphoreType.DMA((cells - 1,)),
                pltpu.SemaphoreType.DMA((cells - 1,)),
                pltpu.SemaphoreType.DMA((shares - 1,)),
                pltpu.SemaphoreType.DMA((shares - 1,)),
            ],
            compiler_params=pltpu.CompilerParams(
                collective_id=0, has_side_effects=True, vmem_limit_bytes=24 * 1024 * 1024
            ),
        )(*[
            pltpu.with_memory_space_constraint(x, pltpu.HBM)
            for x in (gaussians, tile_lists, list_blocks, cell_order, view_vector, cotangent)
        ])
        return pl.pallas_call(
            finish,
            name="finish",
            out_shape=(
                jax.ShapeDtypeStruct(image.shape, F32),
                jax.ShapeDtypeStruct(rows.shape, F32),
            ),
            in_specs=[vmem] * 2,
            out_specs=(vmem, vmem),
            compiler_params=pltpu.CompilerParams(vmem_limit_bytes=4 * 1024 * 1024),
        )(image, rows)

    placed = (
        P(None, "cell"),
        P("cell", "tile", None),
        P("cell", "tile"),
        P(),
        P(),
        P(None, "tile", None),
    )
    return jax.shard_map(
        on_device,
        mesh=mesh,
        in_specs=placed,
        out_specs=(P(None, "tile", None), P(None, ("cell", "tile"))),
        check_vma=False,
    )
```

```python
import functools

import jax
import jax.numpy as jnp
from jax import lax
from jax.experimental import pallas as pl
from jax.experimental.pallas import tpu as pltpu
from jax.sharding import PartitionSpec as P

TILE_SIDE = 16
LANES = 128
CHUNKS = 4
UNROLL = 8
ROWS = 16
SUBLANES = 8
WIDE = 256
FORM_ROWS = 32
NOTHING = -1e9
LOG2E = 1.4426950408889634
BACKGROUND = 1.0
FOCAL = 6.0
BLUR = 0.3
F32 = jnp.float32
MESH = pl.DeviceIdType.MESH


def harmonic_basis(vx, vy, vz):
    norm = jnp.sqrt(vx * vx + vy * vy + vz * vz)
    x, y, z = vx / norm, vy / norm, vz / norm
    return [
        0.28209479177387814 + 0.0 * x,
        -0.4886025119029199 * y,
        0.4886025119029199 * z,
        -0.4886025119029199 * x,
        1.0925484305920792 * x * y,
        -1.0925484305920792 * y * z,
        0.31539156525252005 * (2.0 * z * z - x * x - y * y),
        -1.0925484305920792 * x * z,
        0.5462742152960396 * (x * x - y * y),
        -0.5900435899266435 * y * (3.0 * x * x - y * y),
        2.890611442640554 * x * y * z,
        -0.4570457994644658 * y * (4.0 * z * z - x * x - y * y),
        0.3731763325901154 * z * (2.0 * z * z - 3.0 * x * x - 3.0 * y * y),
        -0.4570457994644658 * x * (4.0 * z * z - x * x - y * y),
        1.445305721320277 * z * (x * x - y * y),
        -0.5900435899266435 * x * (x * x - 3.0 * y * y),
    ]


def conic(depth, s0, s1, s2, q0, q1, q2, q3):
    scales = [jnp.exp(2.0 * s) for s in (s0, s1, s2)]
    norm = jnp.sqrt(q0 * q0 + q1 * q1 + q2 * q2 + q3 * q3)
    w, a, b, c = q0 / norm, q1 / norm, q2 / norm, q3 / norm
    row_one = (1.0 - 2.0 * (b * b + c * c), 2.0 * (a * b - w * c), 2.0 * (a * c + w * b))
    row_two = (2.0 * (a * b + w * c), 1.0 - 2.0 * (a * a + c * c), 2.0 * (b * c - w * a))
    ratio = FOCAL / depth
    zoom = ratio * ratio
    xx = zoom * sum(row_one[k] * row_one[k] * scales[k] for k in range(3)) + BLUR
    xy = zoom * sum(row_one[k] * row_two[k] * scales[k] for k in range(3))
    yy = zoom * sum(row_two[k] * row_two[k] * scales[k] for k in range(3)) + BLUR
    det = xx * yy - xy * xy
    return yy / det, -xy / det, xx / det


def sigmoid(x):
    return 1.0 / (1.0 + jnp.exp(-x))


def pick(values, lane):
    return jnp.take_along_axis(values, lane, axis=1, mode="promise_in_bounds")


def harmonic_rows(view_ref, first, rows):
    shape = (rows, LANES)
    vx, vy, vz = (jnp.full(shape, view_ref[k], F32) for k in range(3))
    row = lax.broadcasted_iota(jnp.int32, shape, 0)
    out = jnp.zeros(shape, F32)
    for k, value in enumerate(harmonic_basis(vx, vy, vz)):
        out = jnp.where(row == first + k, value, out)
    return out


def project_all(gauss_ref, view_ref, rows_ref, table_ref, loads):
    blocks = gauss_ref.shape[1] // LANES
    weights = harmonic_rows(view_ref, 3, 24)
    for k in range(blocks):
        if k % (blocks // CHUNKS) == 0:
            loads[k // (blocks // CHUNKS)].wait()
        cols = pl.ds(k * LANES, LANES)
        for r in range(11):
            rows_ref[r, pl.ds(k, 1), :] = gauss_ref[pl.ds(r, 1), cols]
        for ch in range(3):
            start = 8 + 16 * ch
            size = min(24, gauss_ref.shape[0] - start)
            part = gauss_ref[pl.ds(start, size), cols] * weights[:size]
            table_ref[6 + ch, pl.ds(k, 1), :] = 0.5 + jnp.sum(part, axis=0, keepdims=True)
    a, b, c = conic(*[rows_ref[r] for r in range(2, 10)])
    table_ref[0] = rows_ref[0]
    table_ref[1] = rows_ref[1]
    table_ref[2] = a
    table_ref[3] = b
    table_ref[4] = c
    table_ref[5] = sigmoid(rows_ref[10])


def entry_of(part, length):
    at = lax.broadcasted_iota(jnp.int32, (SUBLANES, LANES), 1) + part * LANES
    return (at % SUBLANES) * (length // SUBLANES) + at // SUBLANES


def gather_all(lists_ref, blocks_ref, table_ref, index_ref, picked_ref):
    tiles, length = lists_ref.shape[1], lists_ref.shape[2]
    shape = (tiles, LANES)
    row = lax.broadcasted_iota(jnp.int32, shape, 0)
    limit = jnp.zeros(shape, jnp.int32)
    for t in range(tiles):
        limit = jnp.where(row == t, blocks_ref[0, t] * LANES, limit)
    row_of_tile = lax.axis_index("tile")
    centre_x = (row * TILE_SIDE + TILE_SIDE // 2).astype(F32)
    centre_y = jnp.full(shape, row_of_tile * TILE_SIDE + TILE_SIDE // 2, jnp.int32).astype(F32)
    for part in range(length // LANES):
        cols = pl.ds(part * LANES, LANES)
        entry = jnp.broadcast_to(entry_of(part, length)[:1], shape)
        index = jnp.zeros(shape, jnp.int32)
        for source in range(length // LANES):
            moved = pick(lists_ref[0, :, pl.ds(source * LANES, LANES)], entry % LANES)
            index = jnp.where(entry // LANES == source, moved, index)
        index_ref[:, cols] = index
        high = index // LANES
        low = index - high * LANES
        values = [jnp.zeros(shape, F32) for _ in range(9)]
        for k in range(table_ref.shape[1]):
            hit = high == k
            for r in range(9):
                line = jnp.broadcast_to(table_ref[r, pl.ds(k, 1), :], shape)
                values[r] = jnp.where(hit, pick(line, low), values[r])
        values[0] = values[0] - centre_x
        values[1] = values[1] - centre_y
        values[5] = jnp.where(entry < limit, values[5], 0.0)
        for r in range(9):
            picked_ref[r, :, cols] = values[r]


def split(value):
    top = value.astype(jnp.bfloat16)
    return top, (value - top.astype(F32)).astype(jnp.bfloat16)


def dot(a, b):
    return jnp.dot(a, b, preferred_element_type=F32)


def dot_rows(a, b):
    return lax.dot_general(a, b, (((1,), (1,)), ((), ())), preferred_element_type=F32)


def dot_columns(a, b):
    return lax.dot_general(a, b, (((0,), (0,)), ((), ())), preferred_element_type=F32)


def pieces(value, count):
    out = []
    for _ in range(count):
        top = value.astype(jnp.bfloat16).astype(F32)
        out.append(top)
        value = value - top
    return out


def set_rows(ref, tiles, first, values):
    for n, value in enumerate(values):
        for part in range(ref.shape[0]):
            ref[part, pl.ds((first + n) * tiles, tiles), :] = value[:, part * LANES : (part + 1) * LANES]


def rows_of(ref, t, count, tiles):
    halves = [ref.at[part][pl.ds(t, count, stride=tiles), :] for part in range(ref.shape[0])]
    return jnp.concatenate(halves, axis=1).astype(jnp.bfloat16)


def pixel_basis(basis_ref):
    shape = basis_ref.shape
    pixel = lax.broadcasted_iota(jnp.int32, shape, 1)
    row = lax.broadcasted_iota(jnp.int32, shape, 0)
    half = 0.5 * (TILE_SIDE - 1)
    px = (pixel % TILE_SIDE).astype(F32) - half
    py = (pixel // TILE_SIDE).astype(F32) - half
    out = jnp.zeros(shape, F32)
    for n, value in enumerate([jnp.ones_like(px), px, py, px * px, px * py, py * py]):
        out = jnp.where((row % 6 == n) & (row < 18), value, out)
    basis_ref[...] = out.astype(jnp.bfloat16)


def form_all(picked_ref, cot_ref, form_ref, glow_ref):
    tiles = picked_ref.shape[1]
    cx, cy, a, b, c, op = (picked_ref[r] for r in range(6))
    sx = a * cx + b * cy
    sy = b * cx + c * cy
    level = jnp.where(op > 0.0, jnp.log(jnp.maximum(op, 1e-37)), NOTHING)
    forms = [level - 0.5 * (cx * sx + cy * sy), sx, sy, -0.5 * a, -b, -0.5 * c]
    forms = [pieces(value * LOG2E, 3) for value in forms]
    for p in range(3):
        set_rows(form_ref, tiles, 6 * p, [form[p] for form in forms])
    tints = [pieces(picked_ref[6 + ch], 2) for ch in range(3)]
    for n, p in enumerate((0, 0, 1)):
        set_rows(form_ref, tiles, 18 + 3 * n, [tint[p] for tint in tints])
    set_rows(form_ref, tiles, 27, [jnp.zeros_like(cx)] * 5)
    cots = [pieces(cot_ref[ch], 2) for ch in range(3)]
    blank = jnp.zeros_like(cot_ref[0])
    set_rows(glow_ref, tiles, 0, [blank] * 18)
    for n, p in enumerate((0, 1, 0)):
        set_rows(glow_ref, tiles, 18 + 3 * n, [cot[p] for cot in cots])
    set_rows(glow_ref, tiles, 27, [blank] * 5)


def forward(me, form_ref, basis_ref, alpha_ref, weight_ref, parts_ref, crit_ref, tone_ref):
    tiles, length, pixels = alpha_ref.shape
    shape = (SUBLANES, pixels)
    line = lax.broadcasted_iota(jnp.int32, shape, 0)

    def one_tile(t, _):
        form = rows_of(form_ref, t, FORM_ROWS, tiles)
        alpha_ref[t] = jnp.exp2(dot_columns(form, basis_ref[...]))
        through = jnp.ones(shape, F32)
        for v in range(length // SUBLANES):
            rows = pl.ds(v * SUBLANES, SUBLANES)
            weight = alpha_ref[t, rows, :] * through
            weight_ref[t, rows, :] = weight
            through = through - weight
        for d in (1, 2, 4):
            through = jnp.where(line >= d, through * pltpu.roll(through, d, 0), through)
        crit_ref[me, 0, pl.ds(t, 1), :] = through[SUBLANES - 1 :]
        ahead = jnp.where(line >= 1, pltpu.roll(through, 1, 0), 1.0)
        ahead = jnp.concatenate([ahead, ahead], axis=0)
        for v in range(length // ROWS):
            rows = pl.ds(v * ROWS, ROWS)
            weight = weight_ref[t, rows, :] * ahead
            weight_ref[t, rows, :] = weight
            top, rest = split(weight)
            parts_ref[t, 0, rows, :] = top
            parts_ref[t, 1, rows, :] = rest
        tint = form[FORM_ROWS - ROWS :]
        colour = dot(tint, parts_ref[t, 0]) + dot(tint, parts_ref[t, 1])
        skip = 18 - (FORM_ROWS - ROWS)
        for ch in range(3):
            tone_ref[me, ch, pl.ds(t, 1), :] = colour[skip + ch : skip + ch + 1] + colour[skip + 6 + ch : skip + 7 + ch]
        return 0

    lax.fori_loop(0, tiles, one_tile, 0, unroll=UNROLL)


def local_backward(form_ref, glow_ref, alpha_ref, weight_ref, parts_ref, turned_ref, ends_ref):
    tiles, length, pixels = alpha_ref.shape
    shape = (SUBLANES, pixels)
    line = lax.broadcasted_iota(jnp.int32, shape, 0)

    def one_tile(t, _):
        light = dot_columns(rows_of(form_ref, t, FORM_ROWS, tiles), rows_of(glow_ref, t, FORM_ROWS, tiles))
        for p in range(2):
            turned_ref[t, p] = parts_ref[t, p].T
        seen = jnp.zeros(shape, F32)
        keep = jnp.ones(shape, F32)
        for v in reversed(range(length // SUBLANES)):
            rows = pl.ds(v * SUBLANES, SUBLANES)
            alpha = alpha_ref[t, rows, :]
            weight = weight_ref[t, rows, :]
            change = light[v * SUBLANES : (v + 1) * SUBLANES] - seen
            alpha_ref[t, rows, :] = weight * change
            weight_ref[t, rows, :] = weight * keep
            seen = seen + alpha * change
            keep = keep - alpha * keep
        for d in (1, 2, 4):
            inside = line < SUBLANES - d
            seen = jnp.where(inside, seen + keep * pltpu.roll(seen, SUBLANES - d, 0), seen)
            keep = jnp.where(inside, keep * pltpu.roll(keep, SUBLANES - d, 0), keep)
        inside = line < SUBLANES - 1
        ends_ref[t, 0] = jnp.where(inside, pltpu.roll(seen, SUBLANES - 1, 0), 0.0)
        ends_ref[t, 1] = jnp.where(inside, pltpu.roll(keep, SUBLANES - 1, 0), 1.0)
        return 0

    lax.fori_loop(0, tiles, one_tile, 0, unroll=UNROLL)


def mark_all(index_ref, hot_ref, hit_ref):
    tiles, length = index_ref.shape
    low_size, blocks = hot_ref.shape[1], hit_ref.shape[0]
    for t in range(tiles):
        index = index_ref[pl.ds(t, 1), :]
        high = index // low_size
        low = index - high * low_size
        cols = pl.ds(t * length, length)
        line = lax.broadcasted_iota(jnp.int32, (low_size, length), 0)
        hot_ref[cols, :] = jnp.where(line == low, 1.0, 0.0).astype(jnp.bfloat16).T
        hit_ref[:, cols] = jnp.where(lax.broadcasted_iota(jnp.int32, (blocks, length), 0) == high, 1.0, 0.0)


def backward(basis_ref, alpha_ref, weight_ref, turned_ref, ends_ref, scene_ref, tint_ref, slope_ref, moments_ref):
    tiles, length, pixels = alpha_ref.shape
    basis = basis_ref[:ROWS]

    def one_tile(t, _):
        ahead = scene_ref[0, pl.ds(t, 1), :]
        behind = scene_ref[1, pl.ds(t, 1), :]
        under = ahead * (ends_ref[t, 0] + ends_ref[t, 1] * behind)
        under = jnp.concatenate([under, under], axis=0)
        for v in range(length // ROWS):
            rows = pl.ds(v * ROWS, ROWS)
            top, rest = split(ahead * alpha_ref[t, rows, :] - under * weight_ref[t, rows, :])
            slope_ref[t, 0, rows, :] = top
            slope_ref[t, 1, rows, :] = rest
        sums = dot_rows(basis, slope_ref[t, 0]) + dot_rows(basis, slope_ref[t, 1])
        tint = rows_of(tint_ref, t, ROWS, tiles)
        colour = dot(tint, turned_ref[t, 0]) + dot(tint, turned_ref[t, 1])
        here = pl.ds(t, 1)
        for n in range(6):
            moments_ref[n, here, :] = sums[n : n + 1]
        for ch in range(3):
            moments_ref[6 + ch, here, :] = colour[ch : ch + 1] + colour[3 + ch : 4 + ch]
        return 0

    lax.fori_loop(0, tiles, one_tile, 0, unroll=UNROLL)


def scatter_all(picked_ref, moments_ref, grads_ref, spread_ref, hot_ref, hit_ref, share_ref):
    tiles, length = moments_ref.shape[1], moments_ref.shape[2]
    blocks = hit_ref.shape[0]
    cx, cy = picked_ref[0], picked_ref[1]
    m0, mx, my, mxx, mxy, myy = (moments_ref[n] for n in range(6))
    grads_ref[0] = mx - cx * m0
    grads_ref[1] = my - cy * m0
    grads_ref[2] = mxx - 2.0 * cx * mx + cx * cx * m0
    grads_ref[3] = mxy - cx * my - cy * mx + cx * cy * m0
    grads_ref[4] = myy - 2.0 * cy * my + cy * cy * m0
    grads_ref[5] = m0
    for ch in range(3):
        grads_ref[6 + ch] = moments_ref[6 + ch]
    for t in range(tiles):
        cols = pl.ds(t * length, length)
        hit = hit_ref[:, cols]
        for r in range(9):
            top, rest = split(hit * grads_ref[r, pl.ds(t, 1), :])
            rows = pl.ds(r * blocks, blocks)
            spread_ref[rows, cols] = top
            spread_ref[pl.ds((9 + r) * blocks, blocks), cols] = rest
    hot = hot_ref[...]
    total = dot(spread_ref[...], hot)
    total = total[: 9 * blocks] + total[9 * blocks :]
    shares, _, lines, _ = share_ref.shape
    for s in range(shares):
        for r in range(9):
            share_ref[s, r] = total[r * blocks + s * lines : r * blocks + (s + 1) * lines]


def pull_back(gauss_ref, view_ref, own_ref, grads, out_ref):
    lines, width = own_ref.shape[1:]
    base = lax.axis_index("tile") * (lines * width)
    for k in range(lines):
        cols = pl.ds(pl.multiple_of(base + k * width, width), width)
        for r in range(11):
            own_ref[r, pl.ds(k, 1), :] = gauss_ref[pl.ds(r, 1), cols]
    (a, b, c), pull = jax.vjp(conic, *[own_ref[r] for r in range(2, 10)])
    opacity = sigmoid(own_ref[10])
    sx, sy, sxx, sxy, syy, s0 = grads[:6]
    rows = [a * sx + b * sy, b * sx + c * sy]
    rows += list(pull((-0.5 * sxx, -sxy, -0.5 * syy)))
    rows.append(s0 * (1.0 - opacity))
    basis = jnp.concatenate([harmonic_rows(view_ref, 0, 16)] * (width // LANES), axis=1)
    for k in range(lines):
        cols = pl.ds(k * width, width)
        for r in range(11):
            out_ref[pl.ds(r, 1), cols] = rows[r][k : k + 1]
        for ch in range(3):
            out_ref[pl.ds(11 + 16 * ch, 16), cols] = basis * grads[6 + ch][k : k + 1]


def kernel(
    cells, shares,
    gauss_in, lists_in, blocks_in, order_in, view_in, cot_in,
    image_ref, out_ref,
    gauss_ref, lists_ref, blocks_ref, order_ref, view_ref, cot_ref, load_sem,
    rows_ref, table_ref, index_ref, picked_ref, form_ref, glow_ref, basis_ref, alpha_ref, weight_ref, parts_ref, turned_ref, slope_ref,
    ends_ref, scene_ref, tint_ref, crit_ref, tone_ref, moments_ref, grads_ref, spread_ref, hot_ref, hit_ref,
    share_ref, came_ref, own_ref,
    crit_send, crit_recv, tone_send, tone_recv, tile_send, tile_recv,
):
    me = lax.axis_index("cell")
    row_of_tile = lax.axis_index("tile")
    chunk = gauss_ref.shape[1] // CHUNKS
    pairs = [(view_in, view_ref)]
    pairs += [
        (gauss_in.at[:, pl.ds(n * chunk, chunk)], gauss_ref.at[:, pl.ds(n * chunk, chunk)])
        for n in range(CHUNKS)
    ]
    pairs += [(lists_in, lists_ref), (blocks_in, blocks_ref), (cot_in, cot_ref), (order_in, order_ref)]
    loads = [pltpu.make_async_copy(src, dst, load_sem.at[n]) for n, (src, dst) in enumerate(pairs)]
    for load in loads:
        load.start()
    barrier = pltpu.get_barrier_semaphore()
    cell_peers = [lax.rem(me + off, cells) for off in range(1, cells)]
    tile_peers = [lax.rem(row_of_tile + off, shares) for off in range(1, shares)]
    for peer in cell_peers:
        pl.semaphore_signal(barrier, inc=1, device_id=(peer, row_of_tile), device_id_type=MESH)
    for peer in tile_peers:
        pl.semaphore_signal(barrier, inc=1, device_id=(me, peer), device_id_type=MESH)

    pixel_basis(basis_ref)
    loads[0].wait()
    project_all(gauss_ref, view_ref, rows_ref, table_ref, loads[1 : 1 + CHUNKS])
    for load in loads[1 + CHUNKS :]:
        load.wait()
    gather_all(lists_ref, blocks_ref, table_ref, index_ref, picked_ref)
    form_all(picked_ref, cot_ref, form_ref, glow_ref)
    forward(me, form_ref, basis_ref, alpha_ref, weight_ref, parts_ref, crit_ref, tone_ref)
    crit_ref[me, 1] = sum(cot_ref[ch] * tone_ref[me, ch] for ch in range(3))
    pl.semaphore_wait(barrier, cells + shares - 2)
    groups = []
    def send_all(ref, send, recv):
        copies = []
        for n, peer in enumerate(cell_peers):
            copy = pltpu.make_async_remote_copy(
                src_ref=ref.at[me], dst_ref=ref.at[me],
                send_sem=send.at[n], recv_sem=recv.at[n],
                device_id=(peer, row_of_tile), device_id_type=MESH,
            )
            copy.start()
            copies.append(copy)
        return copies

    groups.append(send_all(crit_ref, crit_send, crit_recv))
    local_backward(form_ref, glow_ref, alpha_ref, weight_ref, parts_ref, turned_ref, ends_ref)
    mark_all(index_ref, hot_ref, hit_ref)
    for copy in groups[0]:
        copy.wait()
    groups.append(send_all(tone_ref, tone_send, tone_recv))

    shape = crit_ref.shape[2:]
    light = BACKGROUND * (cot_ref[0] + cot_ref[1] + cot_ref[2])
    behind = jnp.zeros(shape, F32)
    ahead = jnp.ones(shape, F32)
    passed = jnp.zeros(shape, jnp.int32)
    for s in reversed(range(cells)):
        cell = order_ref[s]
        mine = jnp.full(shape, cell, jnp.int32) == me
        kept = crit_ref[cell, 0]
        ahead = jnp.where(passed == 1, ahead * kept, ahead)
        behind = jnp.where(mine, light, behind)
        light = crit_ref[cell, 1] + kept * light
        passed = jnp.where(mine, 1, passed)
    scene_ref[0] = ahead
    scene_ref[1] = behind
    tints = [pieces(ahead * cot_ref[ch], 2) for ch in range(3)]
    for p in range(2):
        set_rows(tint_ref, shape[0], 3 * p, [tint[p] for tint in tints])
    set_rows(tint_ref, shape[0], 6, [jnp.zeros(shape, F32)] * (ROWS - 6))

    backward(basis_ref, alpha_ref, weight_ref, turned_ref, ends_ref, scene_ref, tint_ref, slope_ref, moments_ref)
    scatter_all(picked_ref, moments_ref, grads_ref, spread_ref, hot_ref, hit_ref, share_ref)
    copies = []
    for n, peer in enumerate(tile_peers):
        copy = pltpu.make_async_remote_copy(
            src_ref=share_ref.at[peer], dst_ref=came_ref.at[n],
            send_sem=tile_send.at[n], recv_sem=tile_recv.at[n],
            device_id=(me, peer), device_id_type=MESH,
        )
        copy.start()
        copies.append(copy)
    for copy in groups[1]:
        copy.wait()
    image = [jnp.full(shape, BACKGROUND, F32) for _ in range(3)]
    for s in reversed(range(cells)):
        cell = order_ref[s]
        kept = crit_ref[cell, 0]
        for ch in range(3):
            image[ch] = tone_ref[cell, ch] + kept * image[ch]
    for ch in range(3):
        image_ref[ch] = image[ch]
    for copy in copies:
        copy.wait()
    grads = []
    for r in range(9):
        value = share_ref[row_of_tile, r]
        for n in range(shares - 1):
            value = value + came_ref[n, r]
        grads.append(value)
    pull_back(gauss_ref, view_ref, own_ref, grads, out_ref)


def finish(image_in, rows_in, image_ref, rows_ref):
    image_ref[...] = image_in[...]
    rows_ref[...] = rows_in[...]


def solution(mesh):
    cells, shares = mesh.shape["cell"], mesh.shape["tile"]

    def on_device(gaussians, tile_lists, list_blocks, cell_order, view_vector, cotangent):
        tiles, length = tile_lists.shape[1:]
        pixels = cotangent.shape[2]
        count = gaussians.shape[1]
        blocks = count // LANES
        groups = count // WIDE
        lines = groups // shares
        vmem = pl.BlockSpec(memory_space=pltpu.VMEM)
        image, rows = pl.pallas_call(
            functools.partial(kernel, cells, shares),
            name="splat_step",
            out_shape=(
                jax.ShapeDtypeStruct(cotangent.shape, F32),
                jax.ShapeDtypeStruct((gaussians.shape[0], count // shares), F32),
            ),
            in_specs=[pl.BlockSpec(memory_space=pl.ANY)] * 6,
            out_specs=(vmem, vmem),
            scratch_shapes=[
                pltpu.VMEM(gaussians.shape, F32),
                pltpu.VMEM(tile_lists.shape, jnp.int32),
                pltpu.SMEM(list_blocks.shape, jnp.int32),
                pltpu.SMEM(cell_order.shape, jnp.int32),
                pltpu.SMEM(view_vector.shape, F32),
                pltpu.VMEM(cotangent.shape, F32),
                pltpu.SemaphoreType.DMA((CHUNKS + 5,)),
                pltpu.VMEM((11, blocks, LANES), F32),
                pltpu.VMEM((9, blocks, LANES), F32),
                pltpu.VMEM((tiles, length), jnp.int32),
                pltpu.VMEM((9, tiles, length), F32),
                pltpu.VMEM((length // LANES, FORM_ROWS * tiles, LANES), F32),
                pltpu.VMEM((pixels // LANES, FORM_ROWS * tiles, LANES), F32),
                pltpu.VMEM((FORM_ROWS, pixels), jnp.bfloat16),
                pltpu.VMEM((tiles, length, pixels), F32),
                pltpu.VMEM((tiles, length, pixels), F32),
                pltpu.VMEM((tiles, 2, length, pixels), jnp.bfloat16),
                pltpu.VMEM((tiles, 2, pixels, length), jnp.bfloat16),
                pltpu.VMEM((tiles, 2, length, pixels), jnp.bfloat16),
                pltpu.VMEM((tiles, 2, SUBLANES, pixels), F32),
                pltpu.VMEM((2, tiles, pixels), F32),
                pltpu.VMEM((pixels // LANES, ROWS * tiles, LANES), F32),
                pltpu.VMEM((cells, 2, tiles, pixels), F32),
                pltpu.VMEM((cells, 3, tiles, pixels), F32),
                pltpu.VMEM((9, tiles, length), F32),
                pltpu.VMEM((9, tiles, length), F32),
                pltpu.VMEM((18 * groups, tiles * length), jnp.bfloat16),
                pltpu.VMEM((tiles * length, WIDE), jnp.bfloat16),
                pltpu.VMEM((groups, tiles * length), F32),
                pltpu.VMEM((shares, 9, lines, WIDE), F32),
                pltpu.VMEM((shares - 1, 9, lines, WIDE), F32),
                pltpu.VMEM((11, lines, WIDE), F32),
                pltpu.SemaphoreType.DMA((cells - 1,)),
                pltpu.SemaphoreType.DMA((cells - 1,)),
                pltpu.SemaphoreType.DMA((cells - 1,)),
                pltpu.SemaphoreType.DMA((cells - 1,)),
                pltpu.SemaphoreType.DMA((shares - 1,)),
                pltpu.SemaphoreType.DMA((shares - 1,)),
            ],
            compiler_params=pltpu.CompilerParams(
                collective_id=0, has_side_effects=True, vmem_limit_bytes=24 * 1024 * 1024
            ),
        )(*[
            pltpu.with_memory_space_constraint(x, pltpu.HBM)
            for x in (gaussians, tile_lists, list_blocks, cell_order, view_vector, cotangent)
        ])
        return pl.pallas_call(
            finish,
            name="finish",
            out_shape=(
                jax.ShapeDtypeStruct(image.shape, F32),
                jax.ShapeDtypeStruct(rows.shape, F32),
            ),
            in_specs=[vmem] * 2,
            out_specs=(vmem, vmem),
            compiler_params=pltpu.CompilerParams(vmem_limit_bytes=4 * 1024 * 1024),
        )(image, rows)

    placed = (
        P(None, "cell"),
        P("cell", "tile", None),
        P("cell", "tile"),
        P(),
        P(),
        P(None, "tile", None),
    )
    return jax.shard_map(
        on_device,
        mesh=mesh,
        in_specs=placed,
        out_specs=(P(None, "tile", None), P(None, ("cell", "tile"))),
        check_vma=False,
    )
```
